32 devices in a mesh: batch: 8 (over z, x), mp: 4 (over y, core).
Axes of the slice: x: 2, y: 2, z: 4, core: 2. Of those that a mesh axis runs over, the one named last changes fastest.
Arguments:
- img_feat: bfloat16 [128, 1536], P('batch'), may hold values from -6 to 6
- txt_feat: bfloat16 [128, 1536], P('batch'), may hold values from -6 to 6
- w_img: bfloat16 [1536, 1152], P('batch', 'mp'), may hold values from -0.15625 to 0.15625
- w_txt: bfloat16 [1536, 1152], P('batch', 'mp'), may hold values from -0.15625 to 0.15625
- pair_index: int32 [128], P('batch'), may hold values from 0 to 127, each once
- log_scale: float32 [1], replicated, may hold values from 2 to 2.6
- bias: float32 [1], replicated, may hold values from -6 to -4
Outputs:
- image_grad: float32 [128, 1152], P('batch', 'mp')
- text_grad: float32 [128, 1152], P(('batch', 'mp'))
The draws below stay inside these ranges and needn't reach their ends.
Inputs may be any that keep to these rules, and one draw needn't show every extreme that they name: `pair_index`: each text index appears exactly once.
All inputs are finite; a program needn't handle non-finite values.
Results may differ from the reference program's by a relative error of at most 0.0046.
Values may be sent and summed in bfloat16 or wider, within the bound.
A program may use at most 64 MiB of HBM per device.

```python
import jax
import jax.numpy as jnp
from jax import lax

D = 1536
E = 1152
B_LOC = 16
B_TOT = 128
N_BATCH = 8


def level_of(own_key, dims, pieces, least, top_value):
    factor_of = 1.0
    for position, blocks in pieces:
        heights = jax.random.uniform(jax.random.fold_in(jax.random.fold_in(own_key, 6), position), (blocks,), jnp.float32, least / len(pieces), top_value / len(pieces))
        factor_of = factor_of * jnp.repeat(jnp.exp(heights), dims[position] // blocks).reshape((-1,) + (1,) * (len(dims) - 1 - position))
    return factor_of


def gaussian(own_key, dims, width, most, cuts=(), kind=jnp.bfloat16):
    entries = jax.random.normal(own_key, dims, jnp.float32) * width
    if len(cuts) > 0:
        entries = level_of(own_key, dims, cuts, -0.22, 0.18) * entries
    return jnp.clip(entries, min=-most, max=most).astype(kind)


def setup_inputs(seed: int = 0) -> dict:
    key_list = jax.random.split(jax.random.key(seed), 8)
    return {
        "img_feat": gaussian(key_list[0], (B_TOT, D), 1.0, 6.0, ((0, 8),)),
        "txt_feat": gaussian(key_list[1], (B_TOT, D), 1.0, 6.0, ((0, 8),)),
        "w_img": gaussian(key_list[2], (D, E), D ** -0.5, 0.15625, ((0, 8), (1, 4))),
        "w_txt": gaussian(key_list[3], (D, E), D ** -0.5, 0.15625, ((0, 8), (1, 4))),
        "pair_index": jax.random.permutation(key_list[4], B_TOT).astype(jnp.int32),
        "log_scale": jnp.clip(jax.random.uniform(key_list[5], (1,), jnp.float32, 2.0, 2.6), 2.0, 2.6),
        "bias": jnp.clip(jax.random.uniform(key_list[6], (1,), jnp.float32, -6.0, -4.0), -6.0, -4.0),
    }


epsilon = 1e-06

def embed(feat, weight):
    pre = jnp.dot(feat, weight, preferred_element_type=jnp.float32).astype(jnp.bfloat16)
    values = pre.astype(jnp.float32)
    norm = lax.rsqrt(lax.optimization_barrier(jnp.sum(values * values, axis=1, keepdims=True)) + epsilon)
    return (values * norm).astype(jnp.bfloat16)

def reference(img_feat, txt_feat, w_img, w_txt, pair_index, log_scale, bias):
    image = embed(img_feat, w_img)
    text = embed(txt_feat, w_txt)
    scale = jnp.exp(log_scale[0])
    offset = bias[0]
    span = min(N_BATCH, 32)
    half = span // 2
    img_blocks = image.reshape(N_BATCH, B_LOC, E).astype(jnp.float32)
    txt_blocks = text.reshape(N_BATCH, B_LOC, E).astype(jnp.float32)
    pairing = pair_index.reshape(N_BATCH, B_LOC)
    block_ids = jnp.arange(N_BATCH, dtype=jnp.int32)
    inside = jnp.arange(B_LOC, dtype=jnp.int32)
    highest = lax.Precision.HIGHEST

    def one_offset(carry, step):
        img_total, txt_total = carry
        partner = jnp.roll(txt_blocks, -step, axis=0)
        scores = jnp.einsum('hie,hje->hij', img_blocks, partner, precision=highest)
        logits = scale * scores + offset
        columns = ((block_ids + step) % N_BATCH * B_LOC).astype(jnp.int32)[:, None] + inside[None, :]
        label = jnp.where(pairing[:, :, None] == columns[:, None, :], 1.0, -1.0).astype(jnp.float32)
        coef = (-label * jax.nn.sigmoid(-label * logits)).astype(jnp.bfloat16).astype(jnp.float32)
        img_total = img_total + jnp.einsum('hij,hje->hie', coef, partner, precision=highest)
        back = jnp.einsum('hij,hie->hje', coef, img_blocks, precision=highest)
        txt_total = txt_total + jnp.roll(back, step, axis=0)
        return ((img_total, txt_total), None)
    zeros = jnp.zeros((N_BATCH, B_LOC, E), jnp.float32)
    steps = jnp.arange(-half + 1, half + 1, dtype=jnp.int32)
    (img_total, txt_total), unused = lax.scan(one_offset, (zeros, zeros), steps)
    image_grad = scale * img_total.reshape(B_TOT, E)
    text_grad = scale * txt_total.reshape(B_TOT, E)
    return (image_grad, text_grad)
```

```python
import functools

import jax
import jax.numpy as jnp
from jax import lax
from jax.experimental import pallas as pl
from jax.experimental.pallas import tpu as pltpu
from jax.sharding import PartitionSpec as P

epsilon = 1e-06


def from_behind(value, axis, steps):
    count = lax.axis_size(axis)
    pairs = [(source, (source + steps) % count) for source in range(count)]
    return lax.ppermute(value, axis, pairs)


def normalize(pre):
    values = pre.astype(jnp.float32)
    norm = lax.rsqrt(jnp.sum(values * values, axis=1, keepdims=True) + epsilon)
    return (values * norm).astype(jnp.bfloat16)


def block_update(image, pairing, scale, offset, text, first):
    count = text.shape[0]
    scores = lax.dot_general(
        image, text, (((1,), (1,)), ((), ())), preferred_element_type=jnp.float32
    )
    logits = scale * scores + offset
    columns = first + jnp.arange(count, dtype=jnp.int32)
    label = jnp.where(pairing[:, None] == columns[None, :], 1.0, -1.0).astype(jnp.float32)
    coef = (-label * jax.nn.sigmoid(-label * logits)).astype(jnp.bfloat16)
    image_term = jnp.dot(coef, text, preferred_element_type=jnp.float32)
    text_term = lax.dot_general(
        coef, image, (((0,), (0,)), ((), ())), preferred_element_type=jnp.float32
    )
    return (image_term, text_term)


def windowed(img_feat, txt_feat, w_img, w_txt, pair_index, log_scale, bias):
    rows = img_feat.shape[0]
    cycle_size = lax.axis_size("batch")
    group_size = lax.axis_size("mp")
    here = lax.axis_index("batch")
    member = lax.axis_index("mp")
    piece_rows = rows // group_size
    columns_part = w_img.shape[1]
    width = group_size * columns_part
    span = min(cycle_size, 32)
    half = span // 2
    first = jnp.dot(
        img_feat,
        lax.all_gather(w_img, "batch", axis=0, tiled=True),
        preferred_element_type=jnp.float32,
    )
    second = jnp.dot(
        txt_feat,
        lax.all_gather(w_txt, "batch", axis=0, tiled=True),
        preferred_element_type=jnp.float32,
    )
    full_img, full_txt = (
        lax.all_gather(first.astype(jnp.bfloat16), "mp", axis=1, tiled=True),
        lax.all_gather(second.astype(jnp.bfloat16), "mp", axis=1, tiled=True),
    )
    image = normalize(full_img)
    own_start = member * piece_rows
    text = normalize(lax.dynamic_slice_in_dim(full_txt, own_start, piece_rows, 0))
    scale = jnp.exp(log_scale[0])
    offset = bias[0]
    image_total = jnp.zeros((rows, width), jnp.float32)
    start_grads = jnp.zeros((piece_rows, width), jnp.float32)

    def first_row(anchor):
        return anchor * rows + member * piece_rows

    moving = from_behind(text, "batch", -half)

    def turn(step, carry):
        moving, grads, totals = carry
        anchor = (here + half - step) % cycle_size
        image_term, text_term = block_update(
            image, pair_index, scale, offset, moving, first_row(anchor)
        )
        moving = from_behind(moving, "batch", 1)
        grads = from_behind(grads + text_term, "batch", 1)
        return (moving, grads, totals + image_term)

    moving, grads, image_total = lax.fori_loop(0, span, turn, (moving, start_grads, image_total))
    text_total = from_behind(grads, "batch", -half)
    image_part = lax.psum_scatter(image_total, "mp", scatter_dimension=1, tiled=True)
    return (scale * image_part, scale * text_total)


MESH = pl.DeviceIdType.MESH


def coefficients(scores, matched, scale, offset):
    label = jnp.where(matched, 1.0, -1.0).astype(jnp.float32)
    logits = scale * scores + offset
    return (-label * jax.nn.sigmoid(-label * logits)).astype(jnp.bfloat16)


def full_window_kernel(
    cycle, group, feat, w_img, w_txt, pair, log_scale, bias, image_out, text_out,
    feats, partial, parts, every, squares, scores, pairs, pieces,
    feat_send, feat_recv, part_send, part_recv, every_send, every_recv,
    square_send, square_recv, score_send, score_recv, pair_send, pair_recv,
    piece_send, piece_recv,
):
    here = lax.axis_index("batch")
    member = lax.axis_index("mp")
    rows = pair.shape[0]
    total = cycle * rows
    columns = w_img.shape[1]
    piece_rows = rows // group

    def ahead(d):
        return lax.rem(here + d, cycle)

    def behind(d):
        return lax.rem(here + cycle - d, cycle)

    def mate(e):
        return lax.rem(member + e, group)

    def mate_behind(e):
        return lax.rem(member + group - e, group)

    def copy(src, dst, send, recv, device):
        return pltpu.make_async_remote_copy(
            src_ref=src, dst_ref=dst, send_sem=send, recv_sem=recv,
            device_id=device, device_id_type=MESH,
        )

    barrier = pltpu.get_barrier_semaphore()
    for d in range(1, cycle):
        pl.semaphore_signal(barrier, inc=1, device_id=(ahead(d), member), device_id_type=MESH)
    for e in range(1, group):
        pl.semaphore_signal(barrier, inc=1, device_id=(here, mate(e)), device_id_type=MESH)

    lane = lax.broadcasted_iota(jnp.int32, (rows, total), 1)
    row = lax.broadcasted_iota(jnp.int32, (rows, total), 0)
    own_pair = jnp.broadcast_to(pair[...], (rows, total))
    spread = jnp.where(lane - here * rows == row, own_pair.astype(jnp.float32), 0.0)
    pairs[here] = jnp.broadcast_to(jnp.sum(spread, axis=0, keepdims=True), (8, total))
    pl.semaphore_wait(barrier, cycle + group - 2)

    sends = []
    for d in range(1, cycle):
        c = copy(feat.at[ahead(d)], feats.at[here], feat_send.at[d], feat_recv.at[d], (ahead(d), member))
        c.start()
        sends.append(c)
    for d in range(1, cycle):
        c = copy(pairs.at[here], pairs.at[here], pair_send.at[d], pair_recv.at[d], (ahead(d), member))
        c.start()
        sends.append(c)

    def product(block):
        return (
            jnp.dot(block[:rows], w_img[...], preferred_element_type=jnp.float32),
            jnp.dot(block[rows:], w_txt[...], preferred_element_type=jnp.float32),
        )

    image_sum, text_sum = product(feat[here])
    for d in range(1, cycle):
        source = behind(d)
        copy(feat.at[here], feats.at[source], feat_send.at[d], feat_recv.at[d], (source, member)).wait_recv()
        first, second = product(feats[source])
        partial[source, :rows] = first.astype(jnp.bfloat16)
        partial[source, rows:] = second.astype(jnp.bfloat16)
        c = copy(partial.at[source], parts.at[here], part_send.at[d], part_recv.at[d], (source, member))
        c.start()
        sends.append(c)
    for d in range(1, cycle):
        source = ahead(d)
        copy(partial.at[source], parts.at[source], part_send.at[d], part_recv.at[d], (source, member)).wait_recv()
        image_sum = image_sum + parts[source, :rows].astype(jnp.float32)
        text_sum = text_sum + parts[source, rows:].astype(jnp.float32)

    pre = jnp.concatenate([image_sum, text_sum], axis=0).astype(jnp.bfloat16).astype(jnp.float32)
    squares[member] = jnp.broadcast_to(jnp.sum(pre * pre, axis=1, keepdims=True), (2 * rows, 128))
    for e in range(1, group):
        c = copy(squares.at[member], squares.at[member], square_send.at[e], square_recv.at[e], (here, mate(e)))
        c.start()
        sends.append(c)
    for e in range(1, group):
        source = mate_behind(e)
        copy(squares.at[source], squares.at[source], square_send.at[e], square_recv.at[e], (here, source)).wait_recv()
    square = squares[0]
    for k in range(1, group):
        square = square + squares[k]
    norm = lax.rsqrt(square + epsilon)[:, :1]
    own = (pre * norm).astype(jnp.bfloat16)
    every[here] = own
    for d in range(1, cycle):
        c = copy(every.at[here], every.at[here], every_send.at[d], every_recv.at[d], (ahead(d), member))
        c.start()
        sends.append(c)
    for d in range(1, cycle):
        source = behind(d)
        copy(every.at[source], every.at[source], every_send.at[d], every_recv.at[d], (source, member)).wait_recv()
        copy(pairs.at[source], pairs.at[source], pair_send.at[d], pair_recv.at[d], (source, member)).wait_recv()
    images = every[:, :rows].reshape(total, columns)
    texts = every[:, rows:].reshape(total, columns)
    across = (((1,), (1,)), ((), ()))
    scores[member, :rows] = lax.dot_general(own[:rows], texts, across, preferred_element_type=jnp.float32)
    scores[member, rows:] = lax.dot_general(own[rows:], images, across, preferred_element_type=jnp.float32)
    for e in range(1, group):
        c = copy(scores.at[member], scores.at[member], score_send.at[e], score_recv.at[e], (here, mate(e)))
        c.start()
        sends.append(c)
    scale = jnp.exp(jnp.full((1, 1), log_scale[0], jnp.float32))
    offset = bias[0]
    all_pairs = pairs[0]
    for k in range(1, cycle):
        all_pairs = all_pairs + pairs[k]
    of_texts = jnp.broadcast_to(all_pairs[:1], (rows, total)) == (here * rows + row).astype(jnp.float32)
    of_images = own_pair == lane
    for e in range(1, group):
        source = mate_behind(e)
        copy(scores.at[source], scores.at[source], score_send.at[e], score_recv.at[e], (here, source)).wait_recv()
    score = scores[0]
    for k in range(1, group):
        score = score + scores[k]
    text_coef = coefficients(score[rows:], of_texts, scale, offset)
    text_grad = scale * jnp.dot(text_coef, images, preferred_element_type=jnp.float32)
    for k in range(group):
        pieces[0, k] = text_grad[k * piece_rows:(k + 1) * piece_rows]
    for e in range(1, group):
        c = copy(pieces.at[0, mate(e)], pieces.at[1, member], piece_send.at[e], piece_recv.at[e], (here, mate(e)))
        c.start()
        sends.append(c)
    pieces[1, member] = pieces[0, member]
    image_coef = coefficients(score[:rows], of_images, scale, offset)
    image_out[...] = scale * jnp.dot(image_coef, texts, preferred_element_type=jnp.float32)
    for e in range(1, group):
        source = mate_behind(e)
        copy(pieces.at[0, source], pieces.at[1, source], piece_send.at[e], piece_recv.at[e], (here, source)).wait_recv()
    for k in range(group):
        text_out[:, k * columns:(k + 1) * columns] = pieces[1, k]
    for c in sends:
        c.wait_send()


def full_window(img_feat, txt_feat, w_img, w_txt, pair_index, log_scale, bias):
    cycle = lax.axis_size("batch")
    group = lax.axis_size("mp")
    rows = img_feat.shape[0]
    depth, columns = w_img.shape
    total = cycle * rows
    feat = jnp.concatenate([img_feat, txt_feat], axis=0)
    feat = feat.reshape(2 * rows, cycle, depth).transpose(1, 0, 2)
    vmem = pl.BlockSpec(memory_space=pltpu.VMEM)
    smem = pl.BlockSpec(memory_space=pltpu.SMEM)
    batch_sems = [pltpu.SemaphoreType.DMA((cycle,))] * 2
    group_sems = [pltpu.SemaphoreType.DMA((group,))] * 2
    return pl.pallas_call(
        functools.partial(full_window_kernel, cycle, group),
        out_shape=(
            jax.ShapeDtypeStruct((rows, columns), jnp.float32),
            jax.ShapeDtypeStruct((rows // group, group * columns), jnp.float32),
        ),
        in_specs=[vmem, vmem, vmem, vmem, smem, smem],
        out_specs=(vmem, vmem),
        scratch_shapes=[
            pltpu.VMEM((cycle, 2 * rows, depth), jnp.bfloat16),
            pltpu.VMEM((cycle, 2 * rows, columns), jnp.bfloat16),
            pltpu.VMEM((cycle, 2 * rows, columns), jnp.bfloat16),
            pltpu.VMEM((cycle, 2 * rows, columns), jnp.bfloat16),
            pltpu.VMEM((group, 2 * rows, 128), jnp.float32),
            pltpu.VMEM((group, 2 * rows, total), jnp.float32),
            pltpu.VMEM((cycle, 8, total), jnp.float32),
            pltpu.VMEM((2, group, rows // group, columns), jnp.float32),
        ]
        + batch_sems * 3
        + group_sems * 2
        + batch_sems
        + group_sems,
        compiler_params=pltpu.CompilerParams(collective_id=0, has_side_effects=True),
    )(feat, w_img, w_txt, pair_index.reshape(rows, 1), log_scale, bias)


def local(*operands):
    cycle = lax.axis_size("batch")
    if min(cycle, 32) == cycle:
        return full_window(*operands)
    return windowed(*operands)


def solution(mesh):
    return jax.shard_map(
        local,
        mesh=mesh,
        in_specs=(
            P("batch", None),
            P("batch", None),
            P("batch", "mp"),
            P("batch", "mp"),
            P("batch"),
            P(),
            P(),
        ),
        out_specs=(P("batch", "mp"), P(("batch", "mp"), None)),
        check_vma=False,
    )
```

```python
import functools

import jax
import jax.numpy as jnp
from jax import lax
from jax.experimental import pallas as pl
from jax.experimental.pallas import tpu as pltpu
from jax.sharding import PartitionSpec as P

epsilon = 1e-06


def from_behind(value, axis, steps):
    count = lax.axis_size(axis)
    pairs = [(source, (source + steps) % count) for source in range(count)]
    return lax.ppermute(value, axis, pairs)


def normalize(pre):
    values = pre.astype(jnp.float32)
    norm = lax.rsqrt(jnp.sum(values * values, axis=1, keepdims=True) + epsilon)
    return (values * norm).astype(jnp.bfloat16)


def block_update(image, pairing, scale, offset, text, first):
    count = text.shape[0]
    scores = lax.dot_general(
        image, text, (((1,), (1,)), ((), ())), preferred_element_type=jnp.float32
    )
    logits = scale * scores + offset
    columns = first + jnp.arange(count, dtype=jnp.int32)
    label = jnp.where(pairing[:, None] == columns[None, :], 1.0, -1.0).astype(jnp.float32)
    coef = (-label * jax.nn.sigmoid(-label * logits)).astype(jnp.bfloat16)
    image_term = jnp.dot(coef, text, preferred_element_type=jnp.float32)
    text_term = lax.dot_general(
        coef, image, (((0,), (0,)), ((), ())), preferred_element_type=jnp.float32
    )
    return (image_term, text_term)


def windowed(img_feat, txt_feat, w_img, w_txt, pair_index, log_scale, bias):
    rows = img_feat.shape[0]
    cycle_size = lax.axis_size("batch")
    group_size = lax.axis_size("mp")
    here = lax.axis_index("batch")
    member = lax.axis_index("mp")
    piece_rows = rows // group_size
    columns_part = w_img.shape[1]
    width = group_size * columns_part
    span = min(cycle_size, 32)
    half = span // 2
    first = jnp.dot(
        img_feat,
        lax.all_gather(w_img, "batch", axis=0, tiled=True),
        preferred_element_type=jnp.float32,
    )
    second = jnp.dot(
        txt_feat,
        lax.all_gather(w_txt, "batch", axis=0, tiled=True),
        preferred_element_type=jnp.float32,
    )
    full_img, full_txt = (
        lax.all_gather(first.astype(jnp.bfloat16), "mp", axis=1, tiled=True),
        lax.all_gather(second.astype(jnp.bfloat16), "mp", axis=1, tiled=True),
    )
    image = normalize(full_img)
    own_start = member * piece_rows
    text = normalize(lax.dynamic_slice_in_dim(full_txt, own_start, piece_rows, 0))
    scale = jnp.exp(log_scale[0])
    offset = bias[0]
    image_total = jnp.zeros((rows, width), jnp.float32)
    start_grads = jnp.zeros((piece_rows, width), jnp.float32)

    def first_row(anchor):
        return anchor * rows + member * piece_rows

    moving = from_behind(text, "batch", -half)

    def turn(step, carry):
        moving, grads, totals = carry
        anchor = (here + half - step) % cycle_size
        image_term, text_term = block_update(
            image, pair_index, scale, offset, moving, first_row(anchor)
        )
        moving = from_behind(moving, "batch", 1)
        grads = from_behind(grads + text_term, "batch", 1)
        return (moving, grads, totals + image_term)

    moving, grads, image_total = lax.fori_loop(0, span, turn, (moving, start_grads, image_total))
    text_total = from_behind(grads, "batch", -half)
    image_part = lax.psum_scatter(image_total, "mp", scatter_dimension=1, tiled=True)
    return (scale * image_part, scale * text_total)


MESH = pl.DeviceIdType.MESH


def coefficients(scores, matched, scale, offset):
    label = jnp.where(matched, 1.0, -1.0).astype(jnp.float32)
    logits = scale * scores + offset
    return (-label * jax.nn.sigmoid(-label * logits)).astype(jnp.bfloat16).astype(jnp.float32)


def weighted(coef, block):
    high = coef.astype(jnp.bfloat16)
    low = (coef - high.astype(jnp.float32)).astype(jnp.bfloat16)
    both = jnp.dot(jnp.concatenate([high, low], axis=0), block, preferred_element_type=jnp.float32)
    return both[: coef.shape[0]] + both[coef.shape[0] :]


def cover(depth):
    return -(-depth // 128) * 128


def full_window_kernel(
    cycle, group, img_feat, txt_feat, w_img, w_txt, pair, log_scale, bias, image_out, text_out,
    feat, weight, own_index, own_scale, own_bias, feats, partial, parts, every, squares, scores, norms, pieces,
    stage, feat_send, feat_recv, part_send, part_recv, every_send, every_recv,
    norm_send, norm_recv, square_send, square_recv, score_send, score_recv, piece_send, piece_recv,
):
    here = lax.axis_index("batch")
    member = lax.axis_index("mp")
    rows = img_feat.shape[0]
    total = cycle * rows
    depth, columns = w_img.shape
    width = weight.shape[1]
    spare = width - depth
    piece_rows = rows // group

    def ahead(d):
        return lax.rem(here + d, cycle)

    def behind(d):
        return lax.rem(here + cycle - d, cycle)

    def mate(e):
        return lax.rem(member + e, group)

    def mate_behind(e):
        return lax.rem(member + group - e, group)

    def copy(src, dst, send, recv, device):
        return pltpu.make_async_remote_copy(
            src_ref=src, dst_ref=dst, send_sem=send, recv_sem=recv,
            device_id=device, device_id_type=MESH,
        )

    barrier = pltpu.get_barrier_semaphore()
    for d in range(1, cycle):
        pl.semaphore_signal(barrier, inc=1, device_id=(ahead(d), member), device_id_type=MESH)
    for e in range(1, group):
        pl.semaphore_signal(barrier, inc=1, device_id=(here, mate(e)), device_id_type=MESH)

    shift = lax.rem(here * depth, 128)
    place = pl.ds(pl.multiple_of(shift, 16), depth)
    staged = [
        pltpu.make_async_copy(img_feat, feat.at[0], stage.at[0]),
        pltpu.make_async_copy(txt_feat, feat.at[1], stage.at[1]),
        pltpu.make_async_copy(w_img, weight.at[0, place], stage.at[2]),
        pltpu.make_async_copy(w_txt, weight.at[1, place], stage.at[3]),
        pltpu.make_async_copy(pair, own_index, stage.at[4]),
        pltpu.make_async_copy(log_scale, own_scale, stage.at[5]),
        pltpu.make_async_copy(bias, own_bias, stage.at[6]),
    ]
    for c in staged:
        c.start()
    if spare:
        empty = pl.ds(pl.multiple_of(depth * (1 - lax.div(shift, spare)), 16), spare)
        weight[:, empty] = jnp.zeros((2, spare, columns), jnp.bfloat16)
    for c in staged:
        c.wait()
    pl.semaphore_wait(barrier, cycle + group - 2)

    def columns_of(device):
        start = lax.div(device * depth, 128) * 128
        return feat.at[:, :, pl.ds(pl.multiple_of(start, 128), width)]

    sends = []
    for d in range(1, cycle):
        c = copy(columns_of(ahead(d)), feats.at[here], feat_send.at[d], feat_recv.at[d], (ahead(d), member))
        c.start()
        sends.append(c)

    lane = lax.broadcasted_iota(jnp.int32, (rows, total), 1)
    row = lax.broadcasted_iota(jnp.int32, (rows, total), 0)
    square_lane = lax.broadcasted_iota(jnp.int32, (rows, rows), 1)
    square_row = lax.broadcasted_iota(jnp.int32, (rows, rows), 0)
    index = jnp.broadcast_to(own_index[...].reshape(1, rows), (rows, rows)).astype(jnp.float32)
    index = jnp.sum(jnp.where(square_lane == square_row, index, 0.0), axis=1, keepdims=True)
    mine = lane - here * rows == row

    def spread(column):
        return jnp.sum(jnp.where(mine, jnp.broadcast_to(column, (rows, total)), 0.0), axis=0, keepdims=True)

    def product(block):
        return (
            jnp.dot(block[0], weight[0], preferred_element_type=jnp.float32),
            jnp.dot(block[1], weight[1], preferred_element_type=jnp.float32),
        )

    image_sum, text_sum = product(columns_of(here)[...])
    for d in range(1, cycle):
        source = behind(d)
        copy(columns_of(here), feats.at[source], feat_send.at[d], feat_recv.at[d], (source, member)).wait_recv()
        first, second = product(feats[source])
        partial[source, :rows] = first.astype(jnp.bfloat16)
        partial[source, rows:] = second.astype(jnp.bfloat16)
        c = copy(partial.at[source], parts.at[here], part_send.at[d], part_recv.at[d], (source, member))
        c.start()
        sends.append(c)
    for d in range(1, cycle):
        source = ahead(d)
        copy(partial.at[source], parts.at[source], part_send.at[d], part_recv.at[d], (source, member)).wait_recv()
        image_sum = image_sum + parts[source, :rows].astype(jnp.float32)
        text_sum = text_sum + parts[source, rows:].astype(jnp.float32)

    own = jnp.concatenate([image_sum, text_sum], axis=0).astype(jnp.bfloat16)
    every[here] = own
    for d in range(1, cycle):
        c = copy(every.at[here], every.at[here], every_send.at[d], every_recv.at[d], (ahead(d), member))
        c.start()
        sends.append(c)
    pre = own.astype(jnp.float32)
    squares[member] = jnp.broadcast_to(jnp.sum(pre * pre, axis=1, keepdims=True), (2 * rows, 128))
    for e in range(1, group):
        c = copy(squares.at[member], squares.at[member], square_send.at[e], square_recv.at[e], (here, mate(e)))
        c.start()
        sends.append(c)
    for e in range(1, group):
        source = mate_behind(e)
        copy(squares.at[source], squares.at[source], square_send.at[e], square_recv.at[e], (here, source)).wait_recv()
    square = squares[0]
    for k in range(1, group):
        square = square + squares[k]
    norm = lax.rsqrt(square + epsilon)[:, :1]
    kind = lax.broadcasted_iota(jnp.int32, (8, total), 0)
    norms[here] = jnp.where(
        kind == 0, spread(norm[:rows]), jnp.where(kind == 1, spread(norm[rows:]), spread(index))
    )
    for d in range(1, cycle):
        c = copy(norms.at[here], norms.at[here], norm_send.at[d], norm_recv.at[d], (ahead(d), member))
        c.start()
        sends.append(c)

    for d in range(1, cycle):
        source = behind(d)
        copy(every.at[source], every.at[source], every_send.at[d], every_recv.at[d], (source, member)).wait_recv()
    images = every[:, :rows].reshape(total, columns)
    texts = every[:, rows:].reshape(total, columns)
    across = (((1,), (1,)), ((), ()))
    scores[member, :rows] = lax.dot_general(own[:rows], texts, across, preferred_element_type=jnp.float32)
    scores[member, rows:] = lax.dot_general(own[rows:], images, across, preferred_element_type=jnp.float32)
    for e in range(1, group):
        c = copy(scores.at[member], scores.at[member], score_send.at[e], score_recv.at[e], (here, mate(e)))
        c.start()
        sends.append(c)
    for d in range(1, cycle):
        source = behind(d)
        copy(norms.at[source], norms.at[source], norm_send.at[d], norm_recv.at[d], (source, member)).wait_recv()
    scale = jnp.exp(own_scale[...].reshape(1, 1))
    offset = own_bias[...].reshape(1, 1)
    across_norms = norms[0]
    for k in range(1, cycle):
        across_norms = across_norms + norms[k]
    image_norm, text_norm, indices = across_norms[0:1], across_norms[1:2], across_norms[2:3]
    of_texts = jnp.broadcast_to(indices, (rows, total)) == (here * rows + row).astype(jnp.float32)
    of_images = jnp.broadcast_to(index, (rows, total)) == lane.astype(jnp.float32)
    for e in range(1, group):
        source = mate_behind(e)
        copy(scores.at[source], scores.at[source], score_send.at[e], score_recv.at[e], (here, source)).wait_recv()
    score = scores[0]
    for k in range(1, group):
        score = score + scores[k]
    text_coef = coefficients(score[rows:] * (norm[rows:] * image_norm), of_texts, scale, offset)
    text_grad = scale * weighted(text_coef * image_norm, images)
    for k in range(group):
        pieces[0, k] = text_grad[k * piece_rows : (k + 1) * piece_rows]
    for e in range(1, group):
        c = copy(pieces.at[0, mate(e)], pieces.at[1, member], piece_send.at[e], piece_recv.at[e], (here, mate(e)))
        c.start()
        sends.append(c)
    pieces[1, member] = pieces[0, member]
    image_coef = coefficients(score[:rows] * (norm[:rows] * text_norm), of_images, scale, offset)
    image_out[...] = scale * weighted(image_coef * text_norm, texts)
    for e in range(1, group):
        source = mate_behind(e)
        copy(pieces.at[0, source], pieces.at[1, source], piece_send.at[e], piece_recv.at[e], (here, source)).wait_recv()
    for k in range(group):
        text_out[:, k * columns : (k + 1) * columns] = pieces[1, k]
    for c in sends:
        c.wait_send()


def full_window(img_feat, txt_feat, w_img, w_txt, pair_index, log_scale, bias):
    cycle = lax.axis_size("batch")
    group = lax.axis_size("mp")
    rows, features = img_feat.shape
    depth, columns = w_img.shape
    total = cycle * rows
    width = cover(depth)
    vmem = pl.BlockSpec(memory_space=pltpu.VMEM)
    anywhere = pl.BlockSpec(memory_space=pl.ANY)
    batch_sems = [pltpu.SemaphoreType.DMA((cycle,))] * 2
    group_sems = [pltpu.SemaphoreType.DMA((group,))] * 2
    return pl.pallas_call(
        functools.partial(full_window_kernel, cycle, group),
        out_shape=(
            jax.ShapeDtypeStruct((rows, columns), jnp.float32),
            jax.ShapeDtypeStruct((rows // group, group * columns), jnp.float32),
        ),
        in_specs=[anywhere] * 7,
        out_specs=(vmem, vmem),
        scratch_shapes=[
            pltpu.VMEM((2, rows, features), jnp.bfloat16),
            pltpu.VMEM((2, width, columns), jnp.bfloat16),
            pltpu.VMEM((rows,), jnp.int32),
            pltpu.VMEM((1,), jnp.float32),
            pltpu.VMEM((1,), jnp.float32),
            pltpu.VMEM((cycle, 2, rows, width), jnp.bfloat16),
            pltpu.VMEM((cycle, 2 * rows, columns), jnp.bfloat16),
            pltpu.VMEM((cycle, 2 * rows, columns), jnp.bfloat16),
            pltpu.VMEM((cycle, 2 * rows, columns), jnp.bfloat16),
            pltpu.VMEM((group, 2 * rows, 128), jnp.float32),
            pltpu.VMEM((group, 2 * rows, total), jnp.float32),
            pltpu.VMEM((cycle, 8, total), jnp.float32),
            pltpu.VMEM((2, group, rows // group, columns), jnp.float32),
            pltpu.SemaphoreType.DMA((7,)),
        ]
        + batch_sems * 4
        + group_sems * 3,
        compiler_params=pltpu.CompilerParams(collective_id=0, has_side_effects=True),
    )(img_feat, txt_feat, w_img, w_txt, pair_index, log_scale, bias)


def fits_one_kernel(cycle, rows, features, depth):
    width = cover(depth)
    for device in range(cycle):
        shift = device * depth % 128
        if shift not in (0, width - depth) or device * depth - shift + width > features:
            return False
    return min(cycle, 32) == cycle and rows % 16 == 0 and depth % 16 == 0


def local(*operands):
    cycle = lax.axis_size("batch")
    if fits_one_kernel(cycle, *operands[0].shape, operands[2].shape[0]):
        return full_window(*operands)
    return windowed(*operands)


def solution(mesh):
    return jax.shard_map(
        local,
        mesh=mesh,
        in_specs=(
            P("batch", None),
            P("batch", None),
            P("batch", "mp"),
            P("batch", "mp"),
            P("batch"),
            P(),
            P(),
        ),
        out_specs=(P("batch", "mp"), P(("batch", "mp"), None)),
        check_vma=False,
    )
```

```python
import functools

import jax
import jax.numpy as jnp
from jax import lax
from jax.experimental import pallas as pl
from jax.experimental.pallas import tpu as pltpu
from jax.sharding import PartitionSpec as P

epsilon = 1e-06


def from_behind(value, axis, steps):
    count = lax.axis_size(axis)
    pairs = [(source, (source + steps) % count) for source in range(count)]
    return lax.ppermute(value, axis, pairs)


def normalize(pre):
    values = pre.astype(jnp.float32)
    norm = lax.rsqrt(jnp.sum(values * values, axis=1, keepdims=True) + epsilon)
    return (values * norm).astype(jnp.bfloat16)


def block_update(image, pairing, scale, offset, text, first):
    count = text.shape[0]
    scores = lax.dot_general(
        image, text, (((1,), (1,)), ((), ())), preferred_element_type=jnp.float32
    )
    logits = scale * scores + offset
    columns = first + jnp.arange(count, dtype=jnp.int32)
    label = jnp.where(pairing[:, None] == columns[None, :], 1.0, -1.0).astype(jnp.float32)
    coef = (-label * jax.nn.sigmoid(-label * logits)).astype(jnp.bfloat16)
    image_term = jnp.dot(coef, text, preferred_element_type=jnp.float32)
    text_term = lax.dot_general(
        coef, image, (((0,), (0,)), ((), ())), preferred_element_type=jnp.float32
    )
    return (image_term, text_term)


def windowed(img_feat, txt_feat, w_img, w_txt, pair_index, log_scale, bias):
    rows = img_feat.shape[0]
    cycle_size = lax.axis_size("batch")
    group_size = lax.axis_size("mp")
    here = lax.axis_index("batch")
    member = lax.axis_index("mp")
    piece_rows = rows // group_size
    columns_part = w_img.shape[1]
    width = group_size * columns_part
    span = min(cycle_size, 32)
    half = span // 2
    first = jnp.dot(
        img_feat,
        lax.all_gather(w_img, "batch", axis=0, tiled=True),
        preferred_element_type=jnp.float32,
    )
    second = jnp.dot(
        txt_feat,
        lax.all_gather(w_txt, "batch", axis=0, tiled=True),
        preferred_element_type=jnp.float32,
    )
    full_img, full_txt = (
        lax.all_gather(first.astype(jnp.bfloat16), "mp", axis=1, tiled=True),
        lax.all_gather(second.astype(jnp.bfloat16), "mp", axis=1, tiled=True),
    )
    image = normalize(full_img)
    own_start = member * piece_rows
    text = normalize(lax.dynamic_slice_in_dim(full_txt, own_start, piece_rows, 0))
    scale = jnp.exp(log_scale[0])
    offset = bias[0]
    image_total = jnp.zeros((rows, width), jnp.float32)
    start_grads = jnp.zeros((piece_rows, width), jnp.float32)

    def first_row(anchor):
        return anchor * rows + member * piece_rows

    moving = from_behind(text, "batch", -half)

    def turn(step, carry):
        moving, grads, totals = carry
        anchor = (here + half - step) % cycle_size
        image_term, text_term = block_update(
            image, pair_index, scale, offset, moving, first_row(anchor)
        )
        moving = from_behind(moving, "batch", 1)
        grads = from_behind(grads + text_term, "batch", 1)
        return (moving, grads, totals + image_term)

    moving, grads, image_total = lax.fori_loop(0, span, turn, (moving, start_grads, image_total))
    text_total = from_behind(grads, "batch", -half)
    image_part = lax.psum_scatter(image_total, "mp", scatter_dimension=1, tiled=True)
    return (scale * image_part, scale * text_total)


MESH = pl.DeviceIdType.MESH


def coefficients(scores, matched, scale, offset):
    label = jnp.where(matched, 1.0, -1.0).astype(jnp.float32)
    logits = scale * scores + offset
    return (-label * jax.nn.sigmoid(-label * logits)).astype(jnp.bfloat16).astype(jnp.float32)


def weighted(coef, block):
    high = coef.astype(jnp.bfloat16)
    low = (coef - high.astype(jnp.float32)).astype(jnp.bfloat16)
    both = jnp.dot(jnp.concatenate([high, low], axis=0), block, preferred_element_type=jnp.float32)
    return both[: coef.shape[0]] + both[coef.shape[0] :]


def full_window_kernel(
    lines, group, img_feat, txt_feat, w_img, w_txt, pair, log_scale, bias, image_out, text_out,
    feat, loaded, own_index, own_scale, own_bias, weight, feats, products, partial, parts, kept, others,
    squares, scores, norms, pairs, halves, pieces, texts,
    stage, feat_send, feat_recv, weight_sem, pair_sem, part_send, part_recv, other_send, other_recv,
    norm_send, norm_recv, square_send, square_recv, score_send, score_recv, half_sem, piece_send, piece_recv,
):
    here = lax.axis_index("batch")
    member = lax.axis_index("mp")
    line = lax.div(here, 2)
    side = lax.rem(here, 2)
    rows = img_feat.shape[0]
    both = 2 * rows
    total = lines * both
    depth, columns = w_img.shape
    width = 2 * depth
    piece_rows = rows // group

    def ahead(d):
        return lax.rem(line + d, lines)

    def behind(d):
        return lax.rem(line + lines - d, lines)

    def mate(e):
        return lax.rem(member + e, group)

    def mate_behind(e):
        return lax.rem(member + group - e, group)

    def side_of(flip):
        return 1 - side if flip else side

    def copy(src, dst, send, recv, device):
        return pltpu.make_async_remote_copy(
            src_ref=src, dst_ref=dst, send_sem=send, recv_sem=recv,
            device_id=device, device_id_type=MESH,
        )

    neighbour = (2 * line + 1 - side, member)
    barrier = pltpu.get_barrier_semaphore()
    hops = [(d, flip) for d in range(lines) for flip in (0, 1) if d or flip]
    for d, flip in hops:
        pl.semaphore_signal(
            barrier, inc=1, device_id=(2 * ahead(d) + side_of(flip), member), device_id_type=MESH
        )
    for e in range(1, group):
        for flip in (0, 1):
            pl.semaphore_signal(
                barrier, inc=1, device_id=(2 * line + side_of(flip), mate(e)), device_id_type=MESH
            )

    staged = [
        pltpu.make_async_copy(img_feat, feat.at[0], stage.at[0]),
        pltpu.make_async_copy(txt_feat, feat.at[1], stage.at[1]),
        pltpu.make_async_copy(w_img, loaded.at[0], stage.at[2]),
        pltpu.make_async_copy(w_txt, loaded.at[1], stage.at[3]),
        pltpu.make_async_copy(pair, own_index, stage.at[4]),
        pltpu.make_async_copy(log_scale, own_scale, stage.at[5]),
        pltpu.make_async_copy(bias, own_bias, stage.at[6]),
    ]
    for c in staged:
        c.start()
    for c in staged:
        c.wait()
    square_lane = lax.broadcasted_iota(jnp.int32, (rows, rows), 1)
    square_row = lax.broadcasted_iota(jnp.int32, (rows, rows), 0)
    index = jnp.broadcast_to(own_index[...].reshape(1, rows), (rows, rows)).astype(jnp.float32)
    index = jnp.sum(jnp.where(square_lane == square_row, index, 0.0), axis=1, keepdims=True)
    pairs[side] = jnp.broadcast_to(index, (rows, total))
    pl.semaphore_wait(barrier, len(hops) + 2 * (group - 1))

    sends = []

    def send(*how):
        c = copy(*how)
        c.start()
        sends.append(c)

    def slab(tower, of_line):
        return feat.at[tower, :, pl.ds(pl.multiple_of(of_line * width, 128), width)]

    for d, flip in hops:
        to = 2 * ahead(d) + side_of(flip)
        k = 2 * d + flip
        send(slab(side_of(flip), ahead(d)), feats.at[here], feat_send.at[k], feat_recv.at[k], (to, member))
    send(loaded.at[1 - side], weight.at[side], weight_sem.at[0], weight_sem.at[1], neighbour)
    send(pairs.at[side], pairs.at[side], pair_sem.at[0], pair_sem.at[1], neighbour)
    feats[here] = slab(side, line)[...]
    weight[side] = loaded[side]
    for d, flip in hops:
        source = 2 * behind(d) + side_of(flip)
        k = 2 * d + flip
        copy(slab(side, line), feats.at[source], feat_send.at[k], feat_recv.at[k], (source, member)).wait_recv()
    copy(
        loaded.at[side], weight.at[1 - side], weight_sem.at[0], weight_sem.at[1], neighbour
    ).wait_recv()
    product = jnp.dot(
        feats[...].reshape(total, width), weight[...].reshape(width, columns), preferred_element_type=jnp.float32
    )
    products[...] = product.reshape(lines, both, columns)
    partial[...] = product.reshape(lines, both, columns).astype(jnp.bfloat16)
    for d in range(1, lines):
        send(
            partial.at[ahead(d)], parts.at[line], part_send.at[d], part_recv.at[d], (2 * ahead(d) + side, member)
        )
    summed = products[line]
    for d in range(1, lines):
        source = behind(d)
        copy(
            partial.at[source], parts.at[source], part_send.at[d], part_recv.at[d], (2 * source + side, member)
        ).wait_recv()
        summed = summed + parts[source].astype(jnp.float32)

    own = summed.astype(jnp.bfloat16)
    kept[...] = own
    for d in range(lines):
        send(kept, others.at[line], other_send.at[d], other_recv.at[d], (2 * ahead(d) + 1 - side, member))
    pre = own.astype(jnp.float32)
    squares[member] = jnp.broadcast_to(jnp.sum(pre * pre, axis=1, keepdims=True), (both, 128))
    for e in range(1, group):
        send(squares.at[member], squares.at[member], square_send.at[e], square_recv.at[e], (here, mate(e)))
    copy(pairs.at[1 - side], pairs.at[1 - side], pair_sem.at[0], pair_sem.at[1], neighbour).wait_recv()
    lane = lax.broadcasted_iota(jnp.int32, (both, total), 1)
    row = lax.broadcasted_iota(jnp.int32, (both, total), 0) + line * both
    wanted = pairs[...].reshape(both, total)

    def spread(block):
        return jnp.sum(jnp.where(lane == row, block, 0.0), axis=0, keepdims=True)

    wanted_row = spread(wanted)
    for e in range(1, group):
        source = mate_behind(e)
        copy(squares.at[source], squares.at[source], square_send.at[e], square_recv.at[e], (here, source)).wait_recv()
    square = squares[0]
    for k in range(1, group):
        square = square + squares[k]
    norm = lax.rsqrt(square + epsilon)[:, :1]
    kind = lax.broadcasted_iota(jnp.int32, (8, total), 0)
    norm_out = norms.at[lines]
    norm_out[...] = jnp.where(kind == 0, spread(jnp.broadcast_to(norm, (both, total))), wanted_row)
    for d in range(lines):
        send(norm_out, norms.at[line], norm_send.at[d], norm_recv.at[d], (2 * ahead(d) + 1 - side, member))

    for d in range(lines):
        source = behind(d)
        copy(
            kept, others.at[source], other_send.at[d], other_recv.at[d], (2 * source + 1 - side, member)
        ).wait_recv()
    block = others[...].reshape(total, columns)
    scores[member] = lax.dot_general(own, block, (((1,), (1,)), ((), ())), preferred_element_type=jnp.float32)
    for e in range(1, group):
        send(scores.at[member], scores.at[member], score_send.at[e], score_recv.at[e], (here, mate(e)))
    for d in range(lines):
        source = behind(d)
        copy(
            norm_out, norms.at[source], norm_send.at[d], norm_recv.at[d], (2 * source + 1 - side, member)
        ).wait_recv()
    scale = jnp.exp(own_scale[...].reshape(1, 1))
    offset = own_bias[...].reshape(1, 1)
    gathered = norms[0]
    for k in range(1, lines):
        gathered = gathered + norms[k]
    other_norm = gathered[0:1]
    left = jnp.where(side == 0, wanted, row.astype(jnp.float32))
    right = jnp.where(side == 0, lane.astype(jnp.float32), jnp.broadcast_to(gathered[1:2], (both, total)))
    matched = left == right
    factor = norm * other_norm
    for e in range(1, group):
        source = mate_behind(e)
        copy(scores.at[source], scores.at[source], score_send.at[e], score_recv.at[e], (here, source)).wait_recv()
    score = scores[0]
    for k in range(1, group):
        score = score + scores[k]
    coef = coefficients(score * factor, matched, scale, offset)
    grad = scale * weighted(coef * other_norm, block)

    half = copy(halves.at[1], halves.at[2], half_sem.at[0], half_sem.at[1], neighbour)
    spots = [(e, flip) for e in range(group) for flip in (0, 1) if e or flip]

    def piece(e, flip):
        return copy(
            pieces.at[side_of(flip), mate(e)], texts.at[member],
            piece_send.at[2 * e + flip], piece_recv.at[2 * e + flip],
            (2 * line + side_of(flip), mate(e)),
        )

    def arrived(e, flip):
        source = mate_behind(e)
        copy(
            pieces.at[side, source], texts.at[source],
            piece_send.at[2 * e + flip], piece_recv.at[2 * e + flip],
            (2 * line + side_of(flip), source),
        ).wait_recv()

    @pl.when(side == 0)
    def _():
        halves[1] = grad[rows:]
        half.start()
        image_out[...] = grad[:rows]
        for e in range(group):
            arrived(e, 1)
        half.wait_send()

    @pl.when(side == 1)
    def _():
        for k in range(2 * group):
            pieces[k // group, k % group] = grad[k * piece_rows : (k + 1) * piece_rows]
        for e, flip in spots:
            piece(e, flip).start()
        texts[member] = pieces[side, member]
        half.wait_recv()
        image_out[...] = halves[2]
        for e in range(1, group):
            arrived(e, 0)
        for e, flip in spots:
            piece(e, flip).wait_send()

    for k in range(group):
        text_out[:, k * columns : (k + 1) * columns] = texts[k]
    for c in sends:
        c.wait_send()


def full_window(img_feat, txt_feat, w_img, w_txt, pair_index, log_scale, bias):
    lines = lax.axis_size("batch") // 2
    group = lax.axis_size("mp")
    rows, features = img_feat.shape
    depth, columns = w_img.shape
    total = 2 * lines * rows
    vmem = pl.BlockSpec(memory_space=pltpu.VMEM)
    anywhere = pl.BlockSpec(memory_space=pl.ANY)

    def sems(count):
        return pltpu.SemaphoreType.DMA((count,))

    return pl.pallas_call(
        functools.partial(full_window_kernel, lines, group),
        out_shape=(
            jax.ShapeDtypeStruct((rows, columns), jnp.float32),
            jax.ShapeDtypeStruct((rows // group, group * columns), jnp.float32),
        ),
        in_specs=[anywhere] * 7,
        out_specs=(vmem, vmem),
        scratch_shapes=[
            pltpu.VMEM((2, rows, features), jnp.bfloat16),
            pltpu.VMEM((2, depth, columns), jnp.bfloat16),
            pltpu.VMEM((rows,), jnp.int32),
            pltpu.VMEM((1,), jnp.float32),
            pltpu.VMEM((1,), jnp.float32),
            pltpu.VMEM((2, depth, columns), jnp.bfloat16),
            pltpu.VMEM((2 * lines, rows, 2 * depth), jnp.bfloat16),
            pltpu.VMEM((lines, 2 * rows, columns), jnp.float32),
            pltpu.VMEM((lines, 2 * rows, columns), jnp.bfloat16),
            pltpu.VMEM((lines, 2 * rows, columns), jnp.bfloat16),
            pltpu.VMEM((2 * rows, columns), jnp.bfloat16),
            pltpu.VMEM((lines, 2 * rows, columns), jnp.bfloat16),
            pltpu.VMEM((group, 2 * rows, 128), jnp.float32),
            pltpu.VMEM((group, 2 * rows, total), jnp.float32),
            pltpu.VMEM((lines + 1, 8, total), jnp.float32),
            pltpu.VMEM((2, rows, total), jnp.float32),
            pltpu.VMEM((3, rows, columns), jnp.float32),
            pltpu.VMEM((2, group, rows // group, columns), jnp.float32),
            pltpu.VMEM((group, rows // group, columns), jnp.float32),
        ]
        + [sems(7), sems(2 * lines), sems(2 * lines), sems(2), sems(2)]
        + [sems(lines)] * 6
        + [sems(group)] * 4
        + [sems(2), sems(2 * group), sems(2 * group)],
        compiler_params=pltpu.CompilerParams(collective_id=0, has_side_effects=True),
    )(img_feat, txt_feat, w_img, w_txt, pair_index, log_scale, bias)


def fits_one_kernel(cycle, group, rows, depth):
    aligned = rows % 16 == 0 and rows % group == 0 and 2 * depth % 128 == 0
    return cycle % 2 == 0 and min(cycle, 32) == cycle and aligned


def local(*operands):
    cycle = lax.axis_size("batch")
    group = lax.axis_size("mp")
    if fits_one_kernel(cycle, group, operands[0].shape[0], operands[2].shape[0]):
        return full_window(*operands)
    return windowed(*operands)


def solution(mesh):
    return jax.shard_map(
        local,
        mesh=mesh,
        in_specs=(
            P("batch", None),
            P("batch", None),
            P("batch", "mp"),
            P("batch", "mp"),
            P("batch"),
            P(),
            P(),
        ),
        out_specs=(P("batch", "mp"), P(("batch", "mp"), None)),
        check_vma=False,
    )
```

```python
import functools

import jax
import jax.numpy as jnp
from jax import lax
from jax.experimental import pallas as pl
from jax.experimental.pallas import tpu as pltpu
from jax.sharding import PartitionSpec as P

epsilon = 1e-06


def from_behind(value, axis, steps):
    count = lax.axis_size(axis)
    pairs = [(source, (source + steps) % count) for source in range(count)]
    return lax.ppermute(value, axis, pairs)


def normalize(pre):
    values = pre.astype(jnp.float32)
    norm = lax.rsqrt(jnp.sum(values * values, axis=1, keepdims=True) + epsilon)
    return (values * norm).astype(jnp.bfloat16)


def block_update(image, pairing, scale, offset, text, first):
    count = text.shape[0]
    scores = lax.dot_general(
        image, text, (((1,), (1,)), ((), ())), preferred_element_type=jnp.float32
    )
    logits = scale * scores + offset
    columns = first + jnp.arange(count, dtype=jnp.int32)
    label = jnp.where(pairing[:, None] == columns[None, :], 1.0, -1.0).astype(jnp.float32)
    coef = (-label * jax.nn.sigmoid(-label * logits)).astype(jnp.bfloat16)
    image_term = jnp.dot(coef, text, preferred_element_type=jnp.float32)
    text_term = lax.dot_general(
        coef, image, (((0,), (0,)), ((), ())), preferred_element_type=jnp.float32
    )
    return (image_term, text_term)


def windowed(img_feat, txt_feat, w_img, w_txt, pair_index, log_scale, bias):
    rows = img_feat.shape[0]
    cycle_size = lax.axis_size("batch")
    group_size = lax.axis_size("mp")
    here = lax.axis_index("batch")
    member = lax.axis_index("mp")
    piece_rows = rows // group_size
    columns_part = w_img.shape[1]
    width = group_size * columns_part
    span = min(cycle_size, 32)
    half = span // 2
    first = jnp.dot(
        img_feat,
        lax.all_gather(w_img, "batch", axis=0, tiled=True),
        preferred_element_type=jnp.float32,
    )
    second = jnp.dot(
        txt_feat,
        lax.all_gather(w_txt, "batch", axis=0, tiled=True),
        preferred_element_type=jnp.float32,
    )
    full_img, full_txt = (
        lax.all_gather(first.astype(jnp.bfloat16), "mp", axis=1, tiled=True),
        lax.all_gather(second.astype(jnp.bfloat16), "mp", axis=1, tiled=True),
    )
    image = normalize(full_img)
    own_start = member * piece_rows
    text = normalize(lax.dynamic_slice_in_dim(full_txt, own_start, piece_rows, 0))
    scale = jnp.exp(log_scale[0])
    offset = bias[0]
    image_total = jnp.zeros((rows, width), jnp.float32)
    start_grads = jnp.zeros((piece_rows, width), jnp.float32)

    def first_row(anchor):
        return anchor * rows + member * piece_rows

    moving = from_behind(text, "batch", -half)

    def turn(step, carry):
        moving, grads, totals = carry
        anchor = (here + half - step) % cycle_size
        image_term, text_term = block_update(
            image, pair_index, scale, offset, moving, first_row(anchor)
        )
        moving = from_behind(moving, "batch", 1)
        grads = from_behind(grads + text_term, "batch", 1)
        return (moving, grads, totals + image_term)

    moving, grads, image_total = lax.fori_loop(0, span, turn, (moving, start_grads, image_total))
    text_total = from_behind(grads, "batch", -half)
    image_part = lax.psum_scatter(image_total, "mp", scatter_dimension=1, tiled=True)
    return (scale * image_part, scale * text_total)


MESH = pl.DeviceIdType.MESH


def coefficients(scores, matched, scale, offset):
    label = jnp.where(matched, 1.0, -1.0).astype(jnp.float32)
    logits = scale * scores + offset
    return (-label * jax.nn.sigmoid(-label * logits)).astype(jnp.bfloat16).astype(jnp.float32)


def weighted(coef, block):
    high = coef.astype(jnp.bfloat16)
    low = (coef - high.astype(jnp.float32)).astype(jnp.bfloat16)
    both = jnp.dot(jnp.concatenate([high, low], axis=0), block, preferred_element_type=jnp.float32)
    return both[: coef.shape[0]] + both[coef.shape[0] :]


def full_window_kernel(
    lines, group, img_feat, txt_feat, w_img, w_txt, pair, log_scale, bias, image_out, text_out,
    feat, loaded, own_index, own_scale, own_bias, weight, feats, products, partial, parts, kept, others,
    squares, scores, norms, pairs, halves, pieces, texts,
    stage, feat_send, feat_recv, weight_sem, pair_sem, part_send, part_recv, other_send, other_recv,
    norm_send, norm_recv, square_send, square_recv, score_send, score_recv, half_sem, piece_send, piece_recv,
):
    here = lax.axis_index("batch")
    member = lax.axis_index("mp")
    line = lax.div(here, 2)
    side = lax.rem(here, 2)
    rows = img_feat.shape[0]
    both = 2 * rows
    total = lines * both
    depth, columns = w_img.shape
    width = 2 * depth
    piece_rows = rows // group

    def ahead(d):
        return lax.rem(line + d, lines)

    def behind(d):
        return lax.rem(line + lines - d, lines)

    def mate(e):
        return lax.rem(member + e, group)

    def mate_behind(e):
        return lax.rem(member + group - e, group)

    def distant(k):
        low = k + jnp.where(k >= line, 1, 0)
        high = lines - 1 - k
        high = high - jnp.where(high <= line, 1, 0)
        to = jnp.where(2 * line >= lines, low, high)
        return to, lax.rem(to + lines - line, lines)

    def side_of(flip):
        return 1 - side if flip else side

    def copy(src, dst, send, recv, device):
        return pltpu.make_async_remote_copy(
            src_ref=src, dst_ref=dst, send_sem=send, recv_sem=recv,
            device_id=device, device_id_type=MESH,
        )

    neighbour = (2 * line + 1 - side, member)
    barrier = pltpu.get_barrier_semaphore()
    hops = [(d, flip) for d in range(lines) for flip in (0, 1) if d or flip]
    for d, flip in hops:
        pl.semaphore_signal(
            barrier, inc=1, device_id=(2 * ahead(d) + side_of(flip), member), device_id_type=MESH
        )
    for e in range(1, group):
        for flip in (0, 1):
            pl.semaphore_signal(
                barrier, inc=1, device_id=(2 * line + side_of(flip), mate(e)), device_id_type=MESH
            )

    staged = [
        pltpu.make_async_copy(img_feat, feat.at[0], stage.at[0]),
        pltpu.make_async_copy(txt_feat, feat.at[1], stage.at[1]),
        pltpu.make_async_copy(w_img, loaded.at[0], stage.at[2]),
        pltpu.make_async_copy(w_txt, loaded.at[1], stage.at[3]),
        pltpu.make_async_copy(pair, own_index, stage.at[4]),
        pltpu.make_async_copy(log_scale, own_scale, stage.at[5]),
        pltpu.make_async_copy(bias, own_bias, stage.at[6]),
    ]
    for c in staged:
        c.start()
    for c in staged:
        c.wait()
    square_lane = lax.broadcasted_iota(jnp.int32, (rows, rows), 1)
    square_row = lax.broadcasted_iota(jnp.int32, (rows, rows), 0)
    index = jnp.broadcast_to(own_index[...].reshape(1, rows), (rows, rows)).astype(jnp.float32)
    index = jnp.sum(jnp.where(square_lane == square_row, index, 0.0), axis=1, keepdims=True)
    pairs[side] = jnp.broadcast_to(index, (rows, total))
    pl.semaphore_wait(barrier, len(hops) + 2 * (group - 1))

    sends = []

    def send(*how):
        c = copy(*how)
        c.start()
        sends.append(c)

    def slab(tower, of_line):
        return feat.at[tower, :, pl.ds(pl.multiple_of(of_line * width, 128), width)]

    send(loaded.at[1 - side], weight.at[side], weight_sem.at[0], weight_sem.at[1], neighbour)
    for step in range(lines - 1):
        to, d = distant(step)
        for flip in (1, 0):
            k = 2 * d + flip
            send(
                slab(side_of(flip), to), feats.at[here], feat_send.at[k], feat_recv.at[k],
                (2 * to + side_of(flip), member),
            )
    send(slab(1 - side, line), feats.at[here], feat_send.at[1], feat_recv.at[1], neighbour)
    send(pairs.at[side], pairs.at[side], pair_sem.at[0], pair_sem.at[1], neighbour)
    feats[here] = slab(side, line)[...]
    weight[side] = loaded[side]
    for d, flip in hops:
        source = 2 * behind(d) + side_of(flip)
        k = 2 * d + flip
        copy(slab(side, line), feats.at[source], feat_send.at[k], feat_recv.at[k], (source, member)).wait_recv()
    copy(
        loaded.at[side], weight.at[1 - side], weight_sem.at[0], weight_sem.at[1], neighbour
    ).wait_recv()
    product = jnp.dot(
        feats[...].reshape(total, width), weight[...].reshape(width, columns), preferred_element_type=jnp.float32
    )
    products[...] = product.reshape(lines, both, columns)
    partial[...] = product.reshape(lines, both, columns).astype(jnp.bfloat16)
    for step in range(lines - 1):
        to, d = distant(step)
        send(partial.at[to], parts.at[line], part_send.at[d], part_recv.at[d], (2 * to + side, member))
    summed = products[line]
    for d in range(1, lines):
        source = behind(d)
        copy(
            partial.at[source], parts.at[source], part_send.at[d], part_recv.at[d], (2 * source + side, member)
        ).wait_recv()
        summed = summed + parts[source].astype(jnp.float32)

    own = summed.astype(jnp.bfloat16)
    kept[...] = own
    for step in range(lines - 1):
        to, d = distant(step)
        send(kept, others.at[line], other_send.at[d], other_recv.at[d], (2 * to + 1 - side, member))
    send(kept, others.at[line], other_send.at[0], other_recv.at[0], neighbour)
    pre = own.astype(jnp.float32)
    squares[member] = jnp.broadcast_to(jnp.sum(pre * pre, axis=1, keepdims=True), (both, 128))
    for e in range(1, group):
        send(squares.at[member], squares.at[member], square_send.at[e], square_recv.at[e], (here, mate(e)))
    copy(pairs.at[1 - side], pairs.at[1 - side], pair_sem.at[0], pair_sem.at[1], neighbour).wait_recv()
    lane = lax.broadcasted_iota(jnp.int32, (both, total), 1)
    row = lax.broadcasted_iota(jnp.int32, (both, total), 0) + line * both
    wanted = pairs[...].reshape(both, total)

    def spread(block):
        return jnp.sum(jnp.where(lane == row, block, 0.0), axis=0, keepdims=True)

    wanted_row = spread(wanted)
    for e in range(1, group):
        source = mate_behind(e)
        copy(squares.at[source], squares.at[source], square_send.at[e], square_recv.at[e], (here, source)).wait_recv()
    square = squares[0]
    for k in range(1, group):
        square = square + squares[k]
    norm = lax.rsqrt(square + epsilon)[:, :1]
    kind = lax.broadcasted_iota(jnp.int32, (8, total), 0)
    norm_out = norms.at[lines]
    norm_out[...] = jnp.where(kind == 0, spread(jnp.broadcast_to(norm, (both, total))), wanted_row)
    for d in range(lines):
        send(norm_out, norms.at[line], norm_send.at[d], norm_recv.at[d], (2 * ahead(d) + 1 - side, member))

    for d in range(lines):
        source = behind(d)
        copy(
            kept, others.at[source], other_send.at[d], other_recv.at[d], (2 * source + 1 - side, member)
        ).wait_recv()
    block = others[...].reshape(total, columns)
    scores[member] = lax.dot_general(own, block, (((1,), (1,)), ((), ())), preferred_element_type=jnp.float32)
    for e in range(1, group):
        send(scores.at[member], scores.at[member], score_send.at[e], score_recv.at[e], (here, mate(e)))
    for d in range(lines):
        source = behind(d)
        copy(
            norm_out, norms.at[source], norm_send.at[d], norm_recv.at[d], (2 * source + 1 - side, member)
        ).wait_recv()
    scale = jnp.exp(own_scale[...].reshape(1, 1))
    offset = own_bias[...].reshape(1, 1)
    gathered = norms[0]
    for k in range(1, lines):
        gathered = gathered + norms[k]
    other_norm = gathered[0:1]
    left = jnp.where(side == 0, wanted, row.astype(jnp.float32))
    right = jnp.where(side == 0, lane.astype(jnp.float32), jnp.broadcast_to(gathered[1:2], (both, total)))
    matched = left == right
    factor = norm * other_norm
    for e in range(1, group):
        source = mate_behind(e)
        copy(scores.at[source], scores.at[source], score_send.at[e], score_recv.at[e], (here, source)).wait_recv()
    score = scores[0]
    for k in range(1, group):
        score = score + scores[k]
    coef = coefficients(score * factor, matched, scale, offset)
    grad = scale * weighted(coef * other_norm, block)

    half = copy(halves.at[1], halves.at[2], half_sem.at[0], half_sem.at[1], neighbour)
    spots = [(e, flip) for e in range(group) for flip in (0, 1) if e or flip]

    def piece(e, flip):
        return copy(
            pieces.at[side_of(flip), mate(e)], texts.at[member],
            piece_send.at[2 * e + flip], piece_recv.at[2 * e + flip],
            (2 * line + side_of(flip), mate(e)),
        )

    def arrived(e, flip):
        source = mate_behind(e)
        copy(
            pieces.at[side, source], texts.at[source],
            piece_send.at[2 * e + flip], piece_recv.at[2 * e + flip],
            (2 * line + side_of(flip), source),
        ).wait_recv()

    @pl.when(side == 0)
    def _():
        halves[1] = grad[rows:]
        half.start()
        image_out[...] = grad[:rows]
        for e in range(group):
            arrived(e, 1)
        half.wait_send()

    @pl.when(side == 1)
    def _():
        for k in range(2 * group):
            pieces[k // group, k % group] = grad[k * piece_rows : (k + 1) * piece_rows]
        for e, flip in spots:
            piece(e, flip).start()
        texts[member] = pieces[side, member]
        half.wait_recv()
        image_out[...] = halves[2]
        for e in range(1, group):
            arrived(e, 0)
        for e, flip in spots:
            piece(e, flip).wait_send()

    for k in range(group):
        text_out[:, k * columns : (k + 1) * columns] = texts[k]
    for c in sends:
        c.wait_send()


def full_window(img_feat, txt_feat, w_img, w_txt, pair_index, log_scale, bias):
    lines = lax.axis_size("batch") // 2
    group = lax.axis_size("mp")
    rows, features = img_feat.shape
    depth, columns = w_img.shape
    total = 2 * lines * rows
    vmem = pl.BlockSpec(memory_space=pltpu.VMEM)
    anywhere = pl.BlockSpec(memory_space=pl.ANY)

    def sems(count):
        return pltpu.SemaphoreType.DMA((count,))

    return pl.pallas_call(
        functools.partial(full_window_kernel, lines, group),
        out_shape=(
            pltpu.VMEM((rows, columns), jnp.float32),
            pltpu.VMEM((rows // group, group * columns), jnp.float32),
        ),
        in_specs=[anywhere] * 7,
        out_specs=(vmem, vmem),
        scratch_shapes=[
            pltpu.VMEM((2, rows, features), jnp.bfloat16),
            pltpu.VMEM((2, depth, columns), jnp.bfloat16),
            pltpu.VMEM((rows,), jnp.int32),
            pltpu.VMEM((1,), jnp.float32),
            pltpu.VMEM((1,), jnp.float32),
            pltpu.VMEM((2, depth, columns), jnp.bfloat16),
            pltpu.VMEM((2 * lines, rows, 2 * depth), jnp.bfloat16),
            pltpu.VMEM((lines, 2 * rows, columns), jnp.float32),
            pltpu.VMEM((lines, 2 * rows, columns), jnp.bfloat16),
            pltpu.VMEM((lines, 2 * rows, columns), jnp.bfloat16),
            pltpu.VMEM((2 * rows, columns), jnp.bfloat16),
            pltpu.VMEM((lines, 2 * rows, columns), jnp.bfloat16),
            pltpu.VMEM((group, 2 * rows, 128), jnp.float32),
            pltpu.VMEM((group, 2 * rows, total), jnp.float32),
            pltpu.VMEM((lines + 1, 8, total), jnp.float32),
            pltpu.VMEM((2, rows, total), jnp.float32),
            pltpu.VMEM((3, rows, columns), jnp.float32),
            pltpu.VMEM((2, group, rows // group, columns), jnp.float32),
            pltpu.VMEM((group, rows // group, columns), jnp.float32),
        ]
        + [sems(7), sems(2 * lines), sems(2 * lines), sems(2), sems(2)]
        + [sems(lines)] * 6
        + [sems(group)] * 4
        + [sems(2), sems(2 * group), sems(2 * group)],
        compiler_params=pltpu.CompilerParams(collective_id=0, has_side_effects=True),
    )(img_feat, txt_feat, w_img, w_txt, pair_index, log_scale, bias)


def fits_one_kernel(cycle, group, rows, depth):
    aligned = rows % 16 == 0 and rows % group == 0 and 2 * depth % 128 == 0
    return cycle % 2 == 0 and min(cycle, 32) == cycle and aligned


def local(*operands):
    cycle = lax.axis_size("batch")
    group = lax.axis_size("mp")
    if fits_one_kernel(cycle, group, operands[0].shape[0], operands[2].shape[0]):
        return full_window(*operands)
    return windowed(*operands)


def solution(mesh):
    return jax.shard_map(
        local,
        mesh=mesh,
        in_specs=(
            P("batch", None),
            P("batch", None),
            P("batch", "mp"),
            P("batch", "mp"),
            P("batch"),
            P(),
            P(),
        ),
        out_specs=(P("batch", "mp"), P(("batch", "mp"), None)),
        check_vma=False,
    )
```

```python
import functools

import jax
import jax.numpy as jnp
from jax import lax
from jax.experimental import pallas as pl
from jax.experimental.pallas import tpu as pltpu
from jax.sharding import PartitionSpec as P

epsilon = 1e-06


def from_behind(value, axis, steps):
    count = lax.axis_size(axis)
    pairs = [(source, (source + steps) % count) for source in range(count)]
    return lax.ppermute(value, axis, pairs)


def normalize(pre):
    values = pre.astype(jnp.float32)
    norm = lax.rsqrt(jnp.sum(values * values, axis=1, keepdims=True) + epsilon)
    return (values * norm).astype(jnp.bfloat16)


def block_update(image, pairing, scale, offset, text, first):
    count = text.shape[0]
    scores = lax.dot_general(
        image, text, (((1,), (1,)), ((), ())), preferred_element_type=jnp.float32
    )
    logits = scale * scores + offset
    columns = first + jnp.arange(count, dtype=jnp.int32)
    label = jnp.where(pairing[:, None] == columns[None, :], 1.0, -1.0).astype(jnp.float32)
    coef = (-label * jax.nn.sigmoid(-label * logits)).astype(jnp.bfloat16)
    image_term = jnp.dot(coef, text, preferred_element_type=jnp.float32)
    text_term = lax.dot_general(
        coef, image, (((0,), (0,)), ((), ())), preferred_element_type=jnp.float32
    )
    return (image_term, text_term)


def windowed(img_feat, txt_feat, w_img, w_txt, pair_index, log_scale, bias):
    rows = img_feat.shape[0]
    cycle_size = lax.axis_size("batch")
    group_size = lax.axis_size("mp")
    here = lax.axis_index("batch")
    member = lax.axis_index("mp")
    piece_rows = rows // group_size
    columns_part = w_img.shape[1]
    width = group_size * columns_part
    span = min(cycle_size, 32)
    half = span // 2
    first = jnp.dot(
        img_feat,
        lax.all_gather(w_img, "batch", axis=0, tiled=True),
        preferred_element_type=jnp.float32,
    )
    second = jnp.dot(
        txt_feat,
        lax.all_gather(w_txt, "batch", axis=0, tiled=True),
        preferred_element_type=jnp.float32,
    )
    full_img, full_txt = (
        lax.all_gather(first.astype(jnp.bfloat16), "mp", axis=1, tiled=True),
        lax.all_gather(second.astype(jnp.bfloat16), "mp", axis=1, tiled=True),
    )
    image = normalize(full_img)
    own_start = member * piece_rows
    text = normalize(lax.dynamic_slice_in_dim(full_txt, own_start, piece_rows, 0))
    scale = jnp.exp(log_scale[0])
    offset = bias[0]
    image_total = jnp.zeros((rows, width), jnp.float32)
    start_grads = jnp.zeros((piece_rows, width), jnp.float32)

    def first_row(anchor):
        return anchor * rows + member * piece_rows

    moving = from_behind(text, "batch", -half)

    def turn(step, carry):
        moving, grads, totals = carry
        anchor = (here + half - step) % cycle_size
        image_term, text_term = block_update(
            image, pair_index, scale, offset, moving, first_row(anchor)
        )
        moving = from_behind(moving, "batch", 1)
        grads = from_behind(grads + text_term, "batch", 1)
        return (moving, grads, totals + image_term)

    moving, grads, image_total = lax.fori_loop(0, span, turn, (moving, start_grads, image_total))
    text_total = from_behind(grads, "batch", -half)
    image_part = lax.psum_scatter(image_total, "mp", scatter_dimension=1, tiled=True)
    return (scale * image_part, scale * text_total)


MESH = pl.DeviceIdType.MESH


def coefficients(scores, matched, scale, offset):
    label = jnp.where(matched, 1.0, -1.0).astype(jnp.float32)
    logits = scale * scores + offset
    return (-label * jax.nn.sigmoid(-label * logits)).astype(jnp.bfloat16).astype(jnp.float32)


def weighted(coef, block):
    high = coef.astype(jnp.bfloat16)
    low = (coef - high.astype(jnp.float32)).astype(jnp.bfloat16)
    both = jnp.dot(jnp.concatenate([high, low], axis=0), block, preferred_element_type=jnp.float32)
    return both[: coef.shape[0]] + both[coef.shape[0] :]


def full_window_kernel(
    lines, group, img_feat, txt_feat, w_img, w_txt, pair, log_scale, bias, image_out, text_out,
    feat, loaded, own_index, own_scale, own_bias, weight, tail, feats, products, partial, parts, kept, others,
    squares, scores, norms, pairs, halves, pieces, texts,
    stage, feat_send, feat_recv, weight_sem, tail_sem, pair_sem, part_send, part_recv, other_send, other_recv,
    norm_send, norm_recv, square_send, square_recv, score_send, score_recv, half_sem, piece_send, piece_recv,
):
    here = lax.axis_index("batch")
    member = lax.axis_index("mp")
    line = lax.div(here, 2)
    side = lax.rem(here, 2)
    rows = img_feat.shape[0]
    both = 2 * rows
    total = lines * both
    depth, columns = w_img.shape
    width = 2 * depth
    piece_rows = rows // group

    def ahead(d):
        return lax.rem(line + d, lines)

    def behind(d):
        return lax.rem(line + lines - d, lines)

    def mate(e):
        return lax.rem(member + e, group)

    def mate_behind(e):
        return lax.rem(member + group - e, group)

    def distant(k):
        low = k + jnp.where(k >= line, 1, 0)
        high = lines - 1 - k
        high = high - jnp.where(high <= line, 1, 0)
        to = jnp.where(2 * line >= lines, low, high)
        return to, lax.rem(to + lines - line, lines)

    def side_of(flip):
        return 1 - side if flip else side

    def copy(src, dst, send, recv, device):
        return pltpu.make_async_remote_copy(
            src_ref=src, dst_ref=dst, send_sem=send, recv_sem=recv,
            device_id=device, device_id_type=MESH,
        )

    neighbour = (2 * line + 1 - side, member)
    barrier = pltpu.get_barrier_semaphore()
    hops = [(d, flip) for d in range(lines) for flip in (0, 1) if d or flip]
    for d, flip in hops:
        pl.semaphore_signal(
            barrier, inc=1, device_id=(2 * ahead(d) + side_of(flip), member), device_id_type=MESH
        )
    for e in range(1, group):
        for flip in (0, 1):
            pl.semaphore_signal(
                barrier, inc=1, device_id=(2 * line + side_of(flip), mate(e)), device_id_type=MESH
            )

    staged = [
        pltpu.make_async_copy(img_feat, feat.at[0], stage.at[0]),
        pltpu.make_async_copy(txt_feat, feat.at[1], stage.at[1]),
        pltpu.make_async_copy(w_img, loaded.at[0], stage.at[2]),
        pltpu.make_async_copy(w_txt, loaded.at[1], stage.at[3]),
        pltpu.make_async_copy(pair, own_index, stage.at[4]),
        pltpu.make_async_copy(log_scale, own_scale, stage.at[5]),
        pltpu.make_async_copy(bias, own_bias, stage.at[6]),
    ]
    for c in staged:
        c.start()
    for c in staged:
        c.wait()
    square_lane = lax.broadcasted_iota(jnp.int32, (rows, rows), 1)
    square_row = lax.broadcasted_iota(jnp.int32, (rows, rows), 0)
    index = jnp.broadcast_to(own_index[...].reshape(1, rows), (rows, rows)).astype(jnp.float32)
    index = jnp.sum(jnp.where(square_lane == square_row, index, 0.0), axis=1, keepdims=True)
    pairs[side] = jnp.broadcast_to(index, (rows, total))
    whole = columns // 128 * 128
    rest = columns - whole
    packs = 128 // rest if rest else 1
    pack_rows = depth // packs
    if rest:
        away = jnp.where(side == 0, loaded[1, :, whole:], loaded[0, :, whole:])
        tail[side] = jnp.concatenate(
            [away[k * pack_rows : (k + 1) * pack_rows] for k in range(packs)], axis=1
        )
    pl.semaphore_wait(barrier, len(hops) + 2 * (group - 1))

    sends = []

    def send(*how):
        c = copy(*how)
        c.start()
        sends.append(c)

    def slab(tower, of_line):
        return feat.at[tower, :, pl.ds(pl.multiple_of(of_line * width, 128), width)]

    send(
        loaded.at[1 - side, :, :whole], weight.at[side, :, :whole], weight_sem.at[0], weight_sem.at[1], neighbour
    )
    if rest:
        send(tail.at[side], tail.at[side], tail_sem.at[0], tail_sem.at[1], neighbour)
    for step in range(lines - 1):
        to, d = distant(step)
        for flip in (1, 0):
            k = 2 * d + flip
            send(
                slab(side_of(flip), to), feats.at[here], feat_send.at[k], feat_recv.at[k],
                (2 * to + side_of(flip), member),
            )
    send(slab(1 - side, line), feats.at[here], feat_send.at[1], feat_recv.at[1], neighbour)
    send(pairs.at[side], pairs.at[side], pair_sem.at[0], pair_sem.at[1], neighbour)
    feats[here] = slab(side, line)[...]
    weight[side] = loaded[side]
    for d, flip in hops:
        source = 2 * behind(d) + side_of(flip)
        k = 2 * d + flip
        copy(slab(side, line), feats.at[source], feat_send.at[k], feat_recv.at[k], (source, member)).wait_recv()
    copy(
        loaded.at[side, :, :whole], weight.at[1 - side, :, :whole], weight_sem.at[0], weight_sem.at[1], neighbour
    ).wait_recv()
    if rest:
        copy(tail.at[1 - side], tail.at[1 - side], tail_sem.at[0], tail_sem.at[1], neighbour).wait_recv()
        packed = tail[1 - side]
        for k in range(packs):
            weight[1 - side, k * pack_rows : (k + 1) * pack_rows, whole:] = packed[:, k * rest : (k + 1) * rest]
    product = jnp.dot(
        feats[...].reshape(total, width), weight[...].reshape(width, columns), preferred_element_type=jnp.float32
    )
    products[...] = product.reshape(lines, both, columns)
    partial[...] = product.reshape(lines, both, columns).astype(jnp.bfloat16)
    for step in range(lines - 1):
        to, d = distant(step)
        send(partial.at[to], parts.at[line], part_send.at[d], part_recv.at[d], (2 * to + side, member))
    summed = products[line]
    for d in range(1, lines):
        source = behind(d)
        copy(
            partial.at[source], parts.at[source], part_send.at[d], part_recv.at[d], (2 * source + side, member)
        ).wait_recv()
        summed = summed + parts[source].astype(jnp.float32)

    own = summed.astype(jnp.bfloat16)
    kept[...] = own
    for step in range(lines - 1):
        to, d = distant(step)
        send(kept, others.at[line], other_send.at[d], other_recv.at[d], (2 * to + 1 - side, member))
    send(kept, others.at[line], other_send.at[0], other_recv.at[0], neighbour)
    pre = own.astype(jnp.float32)
    squares[member] = jnp.broadcast_to(jnp.sum(pre * pre, axis=1, keepdims=True), (both, 128))
    for e in range(1, group):
        send(squares.at[member], squares.at[member], square_send.at[e], square_recv.at[e], (here, mate(e)))
    copy(pairs.at[1 - side], pairs.at[1 - side], pair_sem.at[0], pair_sem.at[1], neighbour).wait_recv()
    lane = lax.broadcasted_iota(jnp.int32, (both, total), 1)
    row = lax.broadcasted_iota(jnp.int32, (both, total), 0) + line * both
    wanted = pairs[...].reshape(both, total)

    def spread(block):
        return jnp.sum(jnp.where(lane == row, block, 0.0), axis=0, keepdims=True)

    wanted_row = spread(wanted)
    for e in range(1, group):
        source = mate_behind(e)
        copy(squares.at[source], squares.at[source], square_send.at[e], square_recv.at[e], (here, source)).wait_recv()
    square = squares[0]
    for k in range(1, group):
        square = square + squares[k]
    norm = lax.rsqrt(square + epsilon)[:, :1]
    kind = lax.broadcasted_iota(jnp.int32, (8, total), 0)
    norm_out = norms.at[lines]
    norm_out[...] = jnp.where(kind == 0, spread(jnp.broadcast_to(norm, (both, total))), wanted_row)
    for d in range(lines):
        send(norm_out, norms.at[line], norm_send.at[d], norm_recv.at[d], (2 * ahead(d) + 1 - side, member))

    for d in range(lines):
        source = behind(d)
        copy(
            kept, others.at[source], other_send.at[d], other_recv.at[d], (2 * source + 1 - side, member)
        ).wait_recv()
    block = others[...].reshape(total, columns)
    scores[member] = lax.dot_general(own, block, (((1,), (1,)), ((), ())), preferred_element_type=jnp.float32)
    for e in range(1, group):
        send(scores.at[member], scores.at[member], score_send.at[e], score_recv.at[e], (here, mate(e)))
    for d in range(lines):
        source = behind(d)
        copy(
            norm_out, norms.at[source], norm_send.at[d], norm_recv.at[d], (2 * source + 1 - side, member)
        ).wait_recv()
    scale = jnp.exp(own_scale[...].reshape(1, 1))
    offset = own_bias[...].reshape(1, 1)
    gathered = norms[0]
    for k in range(1, lines):
        gathered = gathered + norms[k]
    other_norm = gathered[0:1]
    left = jnp.where(side == 0, wanted, row.astype(jnp.float32))
    right = jnp.where(side == 0, lane.astype(jnp.float32), jnp.broadcast_to(gathered[1:2], (both, total)))
    matched = left == right
    factor = norm * other_norm
    for e in range(1, group):
        source = mate_behind(e)
        copy(scores.at[source], scores.at[source], score_send.at[e], score_recv.at[e], (here, source)).wait_recv()
    score = scores[0]
    for k in range(1, group):
        score = score + scores[k]
    coef = coefficients(score * factor, matched, scale, offset)
    grad = scale * weighted(coef * other_norm, block)

    half = copy(halves.at[1], halves.at[2], half_sem.at[0], half_sem.at[1], neighbour)
    spots = [(e, flip) for e in range(group) for flip in (0, 1) if e or flip]

    def piece(e, flip):
        return copy(
            pieces.at[side_of(flip), mate(e)], texts.at[member],
            piece_send.at[2 * e + flip], piece_recv.at[2 * e + flip],
            (2 * line + side_of(flip), mate(e)),
        )

    def arrived(e, flip):
        source = mate_behind(e)
        copy(
            pieces.at[side, source], texts.at[source],
            piece_send.at[2 * e + flip], piece_recv.at[2 * e + flip],
            (2 * line + side_of(flip), source),
        ).wait_recv()

    @pl.when(side == 0)
    def _():
        halves[1] = grad[rows:]
        half.start()
        image_out[...] = grad[:rows]
        for e in range(group):
            arrived(e, 1)
        half.wait_send()

    @pl.when(side == 1)
    def _():
        for k in range(2 * group):
            pieces[k // group, k % group] = grad[k * piece_rows : (k + 1) * piece_rows]
        for e, flip in spots:
            piece(e, flip).start()
        texts[member] = pieces[side, member]
        half.wait_recv()
        image_out[...] = halves[2]
        for e in range(1, group):
            arrived(e, 0)
        for e, flip in spots:
            piece(e, flip).wait_send()

    for k in range(group):
        text_out[:, k * columns : (k + 1) * columns] = texts[k]
    for c in sends:
        c.wait_send()


def full_window(img_feat, txt_feat, w_img, w_txt, pair_index, log_scale, bias):
    lines = lax.axis_size("batch") // 2
    group = lax.axis_size("mp")
    rows, features = img_feat.shape
    depth, columns = w_img.shape
    total = 2 * lines * rows
    vmem = pl.BlockSpec(memory_space=pltpu.VMEM)
    anywhere = pl.BlockSpec(memory_space=pl.ANY)

    def sems(count):
        return pltpu.SemaphoreType.DMA((count,))

    return pl.pallas_call(
        functools.partial(full_window_kernel, lines, group),
        out_shape=(
            pltpu.VMEM((rows, columns), jnp.float32),
            pltpu.VMEM((rows // group, group * columns), jnp.float32),
        ),
        in_specs=[anywhere] * 7,
        out_specs=(vmem, vmem),
        scratch_shapes=[
            pltpu.VMEM((2, rows, features), jnp.bfloat16),
            pltpu.VMEM((2, depth, columns), jnp.bfloat16),
            pltpu.VMEM((rows,), jnp.int32),
            pltpu.VMEM((1,), jnp.float32),
            pltpu.VMEM((1,), jnp.float32),
            pltpu.VMEM((2, depth, columns), jnp.bfloat16),
            pltpu.VMEM((2, depth * (columns % 128) // 128, 128) if columns % 128 else (2, 8, 128), jnp.bfloat16),
            pltpu.VMEM((2 * lines, rows, 2 * depth), jnp.bfloat16),
            pltpu.VMEM((lines, 2 * rows, columns), jnp.float32),
            pltpu.VMEM((lines, 2 * rows, columns), jnp.bfloat16),
            pltpu.VMEM((lines, 2 * rows, columns), jnp.bfloat16),
            pltpu.VMEM((2 * rows, columns), jnp.bfloat16),
            pltpu.VMEM((lines, 2 * rows, columns), jnp.bfloat16),
            pltpu.VMEM((group, 2 * rows, 128), jnp.float32),
            pltpu.VMEM((group, 2 * rows, total), jnp.float32),
            pltpu.VMEM((lines + 1, 8, total), jnp.float32),
            pltpu.VMEM((2, rows, total), jnp.float32),
            pltpu.VMEM((3, rows, columns), jnp.float32),
            pltpu.VMEM((2, group, rows // group, columns), jnp.float32),
            pltpu.VMEM((group, rows // group, columns), jnp.float32),
        ]
        + [sems(7), sems(2 * lines), sems(2 * lines), sems(2), sems(2), sems(2)]
        + [sems(lines)] * 6
        + [sems(group)] * 4
        + [sems(2), sems(2 * group), sems(2 * group)],
        compiler_params=pltpu.CompilerParams(collective_id=0, has_side_effects=True),
    )(img_feat, txt_feat, w_img, w_txt, pair_index, log_scale, bias)


def fits_one_kernel(cycle, group, rows, depth, columns):
    aligned = rows % 16 == 0 and rows % group == 0 and 2 * depth % 128 == 0
    rest = columns % 128
    if rest and (128 % rest or depth % (128 // rest * 16)):
        return False
    return cycle % 2 == 0 and min(cycle, 32) == cycle and aligned


def local(*operands):
    cycle = lax.axis_size("batch")
    group = lax.axis_size("mp")
    if fits_one_kernel(cycle, group, operands[0].shape[0], *operands[2].shape):
        return full_window(*operands)
    return windowed(*operands)


def solution(mesh):
    return jax.shard_map(
        local,
        mesh=mesh,
        in_specs=(
            P("batch", None),
            P("batch", None),
            P("batch", "mp"),
            P("batch", "mp"),
            P("batch"),
            P(),
            P(),
        ),
        out_specs=(P("batch", "mp"), P(("batch", "mp"), None)),
        check_vma=False,
    )
```

```python
import functools

import jax
import jax.numpy as jnp
from jax import lax
from jax.experimental import pallas as pl
from jax.experimental.pallas import tpu as pltpu
from jax.sharding import PartitionSpec as P

epsilon = 1e-06


def from_behind(value, axis, steps):
    count = lax.axis_size(axis)
    pairs = [(source, (source + steps) % count) for source in range(count)]
    return lax.ppermute(value, axis, pairs)


def normalize(pre):
    values = pre.astype(jnp.float32)
    norm = lax.rsqrt(jnp.sum(values * values, axis=1, keepdims=True) + epsilon)
    return (values * norm).astype(jnp.bfloat16)


def block_update(image, pairing, scale, offset, text, first):
    count = text.shape[0]
    scores = lax.dot_general(
        image, text, (((1,), (1,)), ((), ())), preferred_element_type=jnp.float32
    )
    logits = scale * scores + offset
    columns = first + jnp.arange(count, dtype=jnp.int32)
    label = jnp.where(pairing[:, None] == columns[None, :], 1.0, -1.0).astype(jnp.float32)
    coef = (-label * jax.nn.sigmoid(-label * logits)).astype(jnp.bfloat16)
    image_term = jnp.dot(coef, text, preferred_element_type=jnp.float32)
    text_term = lax.dot_general(
        coef, image, (((0,), (0,)), ((), ())), preferred_element_type=jnp.float32
    )
    return (image_term, text_term)


def windowed(img_feat, txt_feat, w_img, w_txt, pair_index, log_scale, bias):
    rows = img_feat.shape[0]
    cycle_size = lax.axis_size("batch")
    group_size = lax.axis_size("mp")
    here = lax.axis_index("batch")
    member = lax.axis_index("mp")
    piece_rows = rows // group_size
    columns_part = w_img.shape[1]
    width = group_size * columns_part
    span = min(cycle_size, 32)
    half = span // 2
    first = jnp.dot(
        img_feat,
        lax.all_gather(w_img, "batch", axis=0, tiled=True),
        preferred_element_type=jnp.float32,
    )
    second = jnp.dot(
        txt_feat,
        lax.all_gather(w_txt, "batch", axis=0, tiled=True),
        preferred_element_type=jnp.float32,
    )
    full_img, full_txt = (
        lax.all_gather(first.astype(jnp.bfloat16), "mp", axis=1, tiled=True),
        lax.all_gather(second.astype(jnp.bfloat16), "mp", axis=1, tiled=True),
    )
    image = normalize(full_img)
    own_start = member * piece_rows
    text = normalize(lax.dynamic_slice_in_dim(full_txt, own_start, piece_rows, 0))
    scale = jnp.exp(log_scale[0])
    offset = bias[0]
    image_total = jnp.zeros((rows, width), jnp.float32)
    start_grads = jnp.zeros((piece_rows, width), jnp.float32)

    def first_row(anchor):
        return anchor * rows + member * piece_rows

    moving = from_behind(text, "batch", -half)

    def turn(step, carry):
        moving, grads, totals = carry
        anchor = (here + half - step) % cycle_size
        image_term, text_term = block_update(
            image, pair_index, scale, offset, moving, first_row(anchor)
        )
        moving = from_behind(moving, "batch", 1)
        grads = from_behind(grads + text_term, "batch", 1)
        return (moving, grads, totals + image_term)

    moving, grads, image_total = lax.fori_loop(0, span, turn, (moving, start_grads, image_total))
    text_total = from_behind(grads, "batch", -half)
    image_part = lax.psum_scatter(image_total, "mp", scatter_dimension=1, tiled=True)
    return (scale * image_part, scale * text_total)


MESH = pl.DeviceIdType.MESH


def coefficients(scores, matched, scale, offset):
    label = jnp.where(matched, 1.0, -1.0).astype(jnp.float32)
    logits = scale * scores + offset
    return (-label * jax.nn.sigmoid(-label * logits)).astype(jnp.bfloat16).astype(jnp.float32)


def weighted(coef, block):
    high = coef.astype(jnp.bfloat16)
    low = (coef - high.astype(jnp.float32)).astype(jnp.bfloat16)
    both = jnp.dot(jnp.concatenate([high, low], axis=0), block, preferred_element_type=jnp.float32)
    return both[: coef.shape[0]] + both[coef.shape[0] :]


def full_window_kernel(
    lines, group, img_feat, txt_feat, w_img, w_txt, pair, log_scale, bias, image_out, text_out,
    feat, loaded, own_index, own_scale, own_bias, weight, tail, feats, products, partial, parts, kept, others,
    squares, scores, norms, pairs, halves, pieces, texts,
    stage, feat_send, feat_recv, weight_sem, tail_sem, pair_sem, part_send, part_recv, other_send, other_recv,
    norm_send, norm_recv, square_send, square_recv, score_send, score_recv, half_sem, piece_send, piece_recv,
):
    here = lax.axis_index("batch")
    member = lax.axis_index("mp")
    line = lax.div(here, 2)
    side = lax.rem(here, 2)
    rows = img_feat.shape[0]
    both = 2 * rows
    total = lines * both
    depth, columns = w_img.shape
    width = 2 * depth
    piece_rows = rows // group

    def ahead(d):
        return lax.rem(line + d, lines)

    def behind(d):
        return lax.rem(line + lines - d, lines)

    def mate(e):
        return lax.rem(member + e, group)

    def mate_behind(e):
        return lax.rem(member + group - e, group)

    def distant(k):
        low = k + jnp.where(k >= line, 1, 0)
        high = lines - 1 - k
        high = high - jnp.where(high <= line, 1, 0)
        to = jnp.where(2 * line >= lines, low, high)
        return to, lax.rem(to + lines - line, lines)

    def side_of(flip):
        return 1 - side if flip else side

    def copy(src, dst, send, recv, device):
        return pltpu.make_async_remote_copy(
            src_ref=src, dst_ref=dst, send_sem=send, recv_sem=recv,
            device_id=device, device_id_type=MESH,
        )

    neighbour = (2 * line + 1 - side, member)
    barrier = pltpu.get_barrier_semaphore()
    hops = [(d, flip) for d in range(lines) for flip in (0, 1) if d or flip]
    for step in range(lines - 1):
        to, d = distant(step)
        for flip in (1, 0):
            pl.semaphore_signal(
                barrier, inc=1, device_id=(2 * to + side_of(flip), member), device_id_type=MESH
            )
    pl.semaphore_signal(barrier, inc=1, device_id=neighbour, device_id_type=MESH)
    for e in range(1, group):
        for flip in (0, 1):
            pl.semaphore_signal(
                barrier, inc=1, device_id=(2 * line + side_of(flip), mate(e)), device_id_type=MESH
            )

    staged = [
        pltpu.make_async_copy(img_feat, feat.at[0], stage.at[0]),
        pltpu.make_async_copy(txt_feat, feat.at[1], stage.at[1]),
        pltpu.make_async_copy(w_img, loaded.at[0], stage.at[2]),
        pltpu.make_async_copy(w_txt, loaded.at[1], stage.at[3]),
        pltpu.make_async_copy(pair, own_index, stage.at[4]),
        pltpu.make_async_copy(log_scale, own_scale, stage.at[5]),
        pltpu.make_async_copy(bias, own_bias, stage.at[6]),
    ]
    for c in staged:
        c.start()
    for c in staged:
        c.wait()
    square_lane = lax.broadcasted_iota(jnp.int32, (rows, rows), 1)
    square_row = lax.broadcasted_iota(jnp.int32, (rows, rows), 0)
    index = jnp.broadcast_to(own_index[...].reshape(1, rows), (rows, rows)).astype(jnp.float32)
    index = jnp.sum(jnp.where(square_lane == square_row, index, 0.0), axis=1, keepdims=True)
    pairs[side] = jnp.broadcast_to(index, (rows, total))
    whole = columns // 128 * 128
    rest = columns - whole
    packs = 128 // rest if rest else 1
    pack_rows = depth // packs
    if rest:
        away = jnp.where(side == 0, loaded[1, :, whole:], loaded[0, :, whole:])
        tail[side] = jnp.concatenate(
            [away[k * pack_rows : (k + 1) * pack_rows] for k in range(packs)], axis=1
        )
    pl.semaphore_wait(barrier, len(hops) + 2 * (group - 1))

    sends = []

    def send(*how):
        c = copy(*how)
        c.start()
        sends.append(c)

    def slab(tower, of_line):
        return feat.at[tower, :, pl.ds(pl.multiple_of(of_line * width, 128), width)]

    send(
        loaded.at[1 - side, :, :whole], weight.at[side, :, :whole], weight_sem.at[0], weight_sem.at[1], neighbour
    )
    if rest:
        send(tail.at[side], tail.at[side], tail_sem.at[0], tail_sem.at[1], neighbour)
    for step in range(lines - 1):
        to, d = distant(step)
        for flip in (1, 0):
            k = 2 * d + flip
            send(
                slab(side_of(flip), to), feats.at[here], feat_send.at[k], feat_recv.at[k],
                (2 * to + side_of(flip), member),
            )
    send(slab(1 - side, line), feats.at[here], feat_send.at[1], feat_recv.at[1], neighbour)
    send(pairs.at[side], pairs.at[side], pair_sem.at[0], pair_sem.at[1], neighbour)
    feats[here] = slab(side, line)[...]
    weight[side] = loaded[side]
    for d, flip in hops:
        source = 2 * behind(d) + side_of(flip)
        k = 2 * d + flip
        copy(slab(side, line), feats.at[source], feat_send.at[k], feat_recv.at[k], (source, member)).wait_recv()
    copy(
        loaded.at[side, :, :whole], weight.at[1 - side, :, :whole], weight_sem.at[0], weight_sem.at[1], neighbour
    ).wait_recv()
    if rest:
        copy(tail.at[1 - side], tail.at[1 - side], tail_sem.at[0], tail_sem.at[1], neighbour).wait_recv()
        packed = tail[1 - side]
        for k in range(packs):
            weight[1 - side, k * pack_rows : (k + 1) * pack_rows, whole:] = packed[:, k * rest : (k + 1) * rest]
    product = jnp.dot(
        feats[...].reshape(total, width), weight[...].reshape(width, columns), preferred_element_type=jnp.float32
    )
    products[...] = product.reshape(lines, both, columns)
    partial[...] = product.reshape(lines, both, columns).astype(jnp.bfloat16)
    for step in range(lines - 1):
        to, d = distant(step)
        send(partial.at[to], parts.at[line], part_send.at[d], part_recv.at[d], (2 * to + side, member))
    summed = products[line]
    for d in range(1, lines):
        source = behind(d)
        copy(
            partial.at[source], parts.at[source], part_send.at[d], part_recv.at[d], (2 * source + side, member)
        ).wait_recv()
        summed = summed + parts[source].astype(jnp.float32)

    own = summed.astype(jnp.bfloat16)
    kept[...] = own
    for step in range(lines - 1):
        to, d = distant(step)
        send(kept, others.at[line], other_send.at[d], other_recv.at[d], (2 * to + 1 - side, member))
    send(kept, others.at[line], other_send.at[0], other_recv.at[0], neighbour)
    pre = own.astype(jnp.float32)
    squares[member] = jnp.broadcast_to(jnp.sum(pre * pre, axis=1, keepdims=True), (both, 128))
    for e in range(1, group):
        send(squares.at[member], squares.at[member], square_send.at[e], square_recv.at[e], (here, mate(e)))
    copy(pairs.at[1 - side], pairs.at[1 - side], pair_sem.at[0], pair_sem.at[1], neighbour).wait_recv()
    lane = lax.broadcasted_iota(jnp.int32, (both, total), 1)
    row = lax.broadcasted_iota(jnp.int32, (both, total), 0) + line * both
    wanted = pairs[...].reshape(both, total)

    def spread(block):
        return jnp.sum(jnp.where(lane == row, block, 0.0), axis=0, keepdims=True)

    wanted_row = spread(wanted)
    for e in range(1, group):
        source = mate_behind(e)
        copy(squares.at[source], squares.at[source], square_send.at[e], square_recv.at[e], (here, source)).wait_recv()
    square = squares[0]
    for k in range(1, group):
        square = square + squares[k]
    norm = lax.rsqrt(square + epsilon)[:, :1]
    kind = lax.broadcasted_iota(jnp.int32, (8, total), 0)
    norm_out = norms.at[lines]
    norm_out[...] = jnp.where(kind == 0, spread(jnp.broadcast_to(norm, (both, total))), wanted_row)
    for step in range(lines - 1):
        to, d = distant(step)
        send(norm_out, norms.at[line], norm_send.at[d], norm_recv.at[d], (2 * to + 1 - side, member))
    send(norm_out, norms.at[line], norm_send.at[0], norm_recv.at[0], neighbour)

    for d in range(lines):
        source = behind(d)
        copy(
            kept, others.at[source], other_send.at[d], other_recv.at[d], (2 * source + 1 - side, member)
        ).wait_recv()
    block = others[...].reshape(total, columns)
    scores[member] = lax.dot_general(own, block, (((1,), (1,)), ((), ())), preferred_element_type=jnp.float32)
    for e in sorted(range(1, group), key=lambda e: abs(2 * e - group)):
        send(scores.at[member], scores.at[member], score_send.at[e], score_recv.at[e], (here, mate(e)))
    for d in range(lines):
        source = behind(d)
        copy(
            norm_out, norms.at[source], norm_send.at[d], norm_recv.at[d], (2 * source + 1 - side, member)
        ).wait_recv()
    scale = jnp.exp(own_scale[...].reshape(1, 1))
    offset = own_bias[...].reshape(1, 1)
    gathered = norms[0]
    for k in range(1, lines):
        gathered = gathered + norms[k]
    other_norm = gathered[0:1]
    left = jnp.where(side == 0, wanted, row.astype(jnp.float32))
    right = jnp.where(side == 0, lane.astype(jnp.float32), jnp.broadcast_to(gathered[1:2], (both, total)))
    matched = left == right
    factor = norm * other_norm
    for e in range(1, group):
        source = mate_behind(e)
        copy(scores.at[source], scores.at[source], score_send.at[e], score_recv.at[e], (here, source)).wait_recv()
    score = scores[0]
    for k in range(1, group):
        score = score + scores[k]
    coef = coefficients(score * factor, matched, scale, offset)
    grad = scale * weighted(coef * other_norm, block)

    half = copy(halves.at[1], halves.at[2], half_sem.at[0], half_sem.at[1], neighbour)
    spots = [(e, flip) for e in range(group) for flip in (0, 1) if e or flip]

    def piece(e, flip):
        return copy(
            pieces.at[side_of(flip), mate(e)], texts.at[member],
            piece_send.at[2 * e + flip], piece_recv.at[2 * e + flip],
            (2 * line + side_of(flip), mate(e)),
        )

    def arrived(e, flip):
        source = mate_behind(e)
        copy(
            pieces.at[side, source], texts.at[source],
            piece_send.at[2 * e + flip], piece_recv.at[2 * e + flip],
            (2 * line + side_of(flip), source),
        ).wait_recv()

    @pl.when(side == 0)
    def _():
        halves[1] = grad[rows:]
        half.start()
        image_out[...] = grad[:rows]
        for e in range(group):
            arrived(e, 1)
        half.wait_send()

    @pl.when(side == 1)
    def _():
        for k in range(2 * group):
            pieces[k // group, k % group] = grad[k * piece_rows : (k + 1) * piece_rows]
        for e, flip in spots:
            piece(e, flip).start()
        texts[member] = pieces[side, member]
        half.wait_recv()
        image_out[...] = halves[2]
        for e in range(1, group):
            arrived(e, 0)
        for e, flip in spots:
            piece(e, flip).wait_send()

    for k in range(group):
        text_out[:, k * columns : (k + 1) * columns] = texts[k]
    for c in sends:
        c.wait_send()


def full_window(img_feat, txt_feat, w_img, w_txt, pair_index, log_scale, bias):
    lines = lax.axis_size("batch") // 2
    group = lax.axis_size("mp")
    rows, features = img_feat.shape
    depth, columns = w_img.shape
    total = 2 * lines * rows
    vmem = pl.BlockSpec(memory_space=pltpu.VMEM)
    anywhere = pl.BlockSpec(memory_space=pl.ANY)

    def sems(count):
        return pltpu.SemaphoreType.DMA((count,))

    return pl.pallas_call(
        functools.partial(full_window_kernel, lines, group),
        out_shape=(
            pltpu.VMEM((rows, columns), jnp.float32),
            pltpu.VMEM((rows // group, group * columns), jnp.float32),
        ),
        in_specs=[anywhere] * 7,
        out_specs=(vmem, vmem),
        scratch_shapes=[
            pltpu.VMEM((2, rows, features), jnp.bfloat16),
            pltpu.VMEM((2, depth, columns), jnp.bfloat16),
            pltpu.VMEM((rows,), jnp.int32),
            pltpu.VMEM((1,), jnp.float32),
            pltpu.VMEM((1,), jnp.float32),
            pltpu.VMEM((2, depth, columns), jnp.bfloat16),
            pltpu.VMEM((2, depth * (columns % 128) // 128, 128) if columns % 128 else (2, 8, 128), jnp.bfloat16),
            pltpu.VMEM((2 * lines, rows, 2 * depth), jnp.bfloat16),
            pltpu.VMEM((lines, 2 * rows, columns), jnp.float32),
            pltpu.VMEM((lines, 2 * rows, columns), jnp.bfloat16),
            pltpu.VMEM((lines, 2 * rows, columns), jnp.bfloat16),
            pltpu.VMEM((2 * rows, columns), jnp.bfloat16),
            pltpu.VMEM((lines, 2 * rows, columns), jnp.bfloat16),
            pltpu.VMEM((group, 2 * rows, 128), jnp.float32),
            pltpu.VMEM((group, 2 * rows, total), jnp.float32),
            pltpu.VMEM((lines + 1, 8, total), jnp.float32),
            pltpu.VMEM((2, rows, total), jnp.float32),
            pltpu.VMEM((3, rows, columns), jnp.float32),
            pltpu.VMEM((2, group, rows // group, columns), jnp.float32),
            pltpu.VMEM((group, rows // group, columns), jnp.float32),
        ]
        + [sems(7), sems(2 * lines), sems(2 * lines), sems(2), sems(2), sems(2)]
        + [sems(lines)] * 6
        + [sems(group)] * 4
        + [sems(2), sems(2 * group), sems(2 * group)],
        compiler_params=pltpu.CompilerParams(collective_id=0, has_side_effects=True),
    )(img_feat, txt_feat, w_img, w_txt, pair_index, log_scale, bias)


def fits_one_kernel(cycle, group, rows, depth, columns):
    aligned = rows % 16 == 0 and rows % group == 0 and 2 * depth % 128 == 0
    rest = columns % 128
    if rest and (128 % rest or depth % (128 // rest * 16)):
        return False
    return cycle % 2 == 0 and min(cycle, 32) == cycle and aligned


def local(*operands):
    cycle = lax.axis_size("batch")
    group = lax.axis_size("mp")
    if fits_one_kernel(cycle, group, operands[0].shape[0], *operands[2].shape):
        return full_window(*operands)
    return windowed(*operands)


def solution(mesh):
    return jax.shard_map(
        local,
        mesh=mesh,
        in_specs=(
            P("batch", None),
            P("batch", None),
            P("batch", "mp"),
            P("batch", "mp"),
            P("batch"),
            P(),
            P(),
        ),
        out_specs=(P("batch", "mp"), P(("batch", "mp"), None)),
        check_vma=False,
    )
```
